32 devices in a mesh: vec: 4 (over z), row: 8 (over y, x, core).
Axes of the slice: x: 2, y: 2, z: 4, core: 2. Of those that a mesh axis runs over, the one named last changes fastest.
Arguments:
- chol_vectors: float32 [128, 1024, 1024], P('vec', 'row'), may hold values from -16 to 16, as said below
Outputs:
- rotated: float32 [128, 1024, 1024], P('vec', 'row')
- rotation: float32 [1024, 1024], P('row')
The draws below stay inside these ranges and needn't reach their ends.
Inputs may be any that keep to these rules, and one draw needn't show every extreme that they name: Every matrix chol_vectors[P] is symmetric in its last two dimensions.
All inputs are finite; a program needn't handle non-finite values.
Results may differ from the reference program's by a relative error of at most 0.00014.
Values sent between devices are 32-bit elements; how exact they have to be, the bound alone decides.
No kernel may reach another device: no remote copies, remote signals or barrier semaphores. Data moves between devices by JAX's collectives and lax.ppermute only.
A program may use at most 128 MiB of HBM per device.

```python
import jax
import jax.numpy as jnp
from jax import lax

N = 1024
ITERS = 2
NP = 128


def draw_chol_vectors(key, part):
    first = jax.random.fold_in(jax.random.fold_in(key, 17), 0)
    values = jax.random.normal(first, (NP, N, N), jnp.float32)
    values = jnp.clip(values, -8.0, 8.0)
    return 0.5 * (values + jnp.transpose(values, (0, 2, 1)))


def setup_inputs(seed: int = 0) -> dict:
    seeds = jax.random.split(jax.random.key(seed), 2)
    chol_vectors = draw_chol_vectors(jax.random.fold_in(seeds[1], 71), 0)
    return dict(chol_vectors=chol_vectors)


def transform(matrix, step):
    left = jnp.dot(matrix, step, precision=lax.Precision.HIGHEST)
    return jnp.dot(left.T, step, precision=lax.Precision.HIGHEST)

def reference(chol_vectors):
    current = chol_vectors
    identity = jnp.eye(N, dtype=jnp.float32)
    rotation = identity
    for iteration in range(ITERS):
        diagonal = jnp.diagonal(current, axis1=1, axis2=2)
        gradient = jnp.einsum('pjk,pj->jk', current, diagonal, precision=lax.Precision.HIGHEST)
        gradient = gradient - jnp.einsum('pjk,pk->jk', current, diagonal, precision=lax.Precision.HIGHEST)
        norm = jnp.sqrt(jnp.sum(gradient * gradient) / (N * N) + 1e-06)
        generator = 0.2 / jnp.sqrt(jnp.float32(N)) * gradient / norm
        step = identity + generator + 0.5 * jnp.dot(generator, generator, precision=lax.Precision.HIGHEST)
        if iteration == 0:
            rotation = step
        else:
            rotation = jnp.dot(rotation, step, precision=lax.Precision.HIGHEST)
        current = lax.map(lambda matrix: transform(matrix, step), current)
    return (current, rotation)
```

```python
import functools

import jax
import jax.numpy as jnp
from jax import lax
from jax.experimental import pallas as pl
from jax.experimental.pallas import tpu as pltpu
from jax.sharding import PartitionSpec as P


step_gain = 0.2
chunk_count = 4
high = lax.Precision.HIGH


def swap(x, k):
    count = lax.axis_size("row")
    return lax.ppermute(x, "row", [(i, i ^ k) for i in range(count)])


def turn(x, k):
    count = lax.axis_size("vec")
    return lax.ppermute(x, "vec", [(i, (i + k) % count) for i in range(count)])


def cut(x, index, size, axis):
    return lax.dynamic_slice_in_dim(x, index * size, size, axis)


def place(whole, part, index):
    return lax.dynamic_update_slice_in_dim(whole, part, index * part.shape[0], 0)


def sum_over_vec(part):
    count = lax.axis_size("vec")
    me = lax.axis_index("vec")
    size = part.shape[0] // count
    total = cut(part, me, size, 0)
    for k in range(1, count):
        total = total + turn(cut(part, (me + k) % count, size, 0), k)
    whole = place(jnp.zeros_like(part), total, me)
    for k in range(1, count):
        whole = place(whole, turn(total, k), (me - k) % count)
    return whole


def gather_rows(part):
    count = lax.axis_size("row")
    me = lax.axis_index("row")
    whole = jnp.zeros((count * part.shape[0], part.shape[1]), part.dtype)
    for k in range(0, count, 2):
        mine = part if k == 0 else swap(part, k)
        whole = place(whole, mine, me ^ k)
        whole = place(whole, swap(mine, 1), me ^ k ^ 1)
    return whole


def sum_over_row(part):
    pair = part + swap(part, 1)
    total = pair
    for k in range(2, lax.axis_size("row"), 2):
        total = total + swap(pair, k)
    return total


def step_of(gradient):
    orbitals = gradient.shape[0]
    norm = jnp.sqrt(jnp.sum(gradient * gradient) / (orbitals * orbitals) + 1e-06)
    generator = step_gain / jnp.sqrt(jnp.float32(orbitals)) * gradient / norm
    square = jnp.dot(generator, generator, precision=high)
    return jnp.eye(orbitals, dtype=jnp.float32) + generator + 0.5 * square


def plain_shards(chol_vectors):
    vectors, rows, orbitals = chol_vectors.shape
    devices = lax.axis_size("row")
    me = lax.axis_index("row")
    chunk = vectors // chunk_count

    block = cut(chol_vectors, me, rows, 2)
    here = jnp.eye(rows, dtype=jnp.bool_)
    diagonal = jnp.sum(jnp.where(here, block, 0.0), axis=2)
    part = jnp.sum(chol_vectors * diagonal[:, :, None], axis=0)
    terms = gather_rows(sum_over_vec(part))
    step = step_of(terms - terms.T)

    step_rows = cut(step, me, rows, 0)
    lefts = []
    part = jnp.zeros((rows, orbitals), jnp.float32)
    for c in range(chunk_count):
        own = chol_vectors[c * chunk : (c + 1) * chunk]
        left = jnp.einsum("pab,bm->pam", own, step, precision=high)
        lefts.append(left)
        diagonal = sum_over_row(jnp.sum(left * step_rows, axis=1))
        part = part + jnp.sum(left * diagonal[:, None, :], axis=0)
    terms = gather_rows(sum_over_vec(part))
    terms = lax.dot_general(step, terms, (((0,), (0,)), ((), ())), precision=high)
    step_next = step_of(terms.T - terms)
    rotation = jnp.dot(step, step_next, precision=high)
    order = me ^ jnp.arange(devices)
    rotation_order = rotation.reshape(devices, rows, orbitals)[order].reshape(orbitals, orbitals)

    outs = []
    for c in range(chunk_count):
        left = jnp.einsum("pab,bm->pam", lefts[c], step_next, precision=high)
        pieces = []
        for k in range(devices):
            piece = cut(left, me ^ k, rows, 2)
            pieces.append(piece if k == 0 else swap(piece, k))
        columns = jnp.concatenate(pieces, axis=1)
        outs.append(jnp.einsum("pam,ak->pmk", columns, rotation_order, precision=high))
    return jnp.concatenate(outs, axis=0), cut(rotation, me, rows, 0)


lane = 128
quad = 4
bf16, f32 = jnp.bfloat16, jnp.float32


def split(x):
    upper = x.astype(bf16)
    return upper, (x - upper.astype(f32)).astype(bf16)


def product(left, right):
    dot = functools.partial(jnp.dot, preferred_element_type=f32)
    return dot(left[0], right[0]) + (dot(left[0], right[1]) + dot(left[1], right[0]))


def whole_spec():
    return pl.BlockSpec(memory_space=pltpu.VMEM)


def resident(shape):
    return pl.BlockSpec(shape, lambda i: (0,) * len(shape), pipeline_mode=pl.Buffered(1))


def cost(flops, data):
    return pl.CostEstimate(flops=flops, bytes_accessed=data, transcendentals=0)


def gradient_kernel(me_ref, vectors_ref, slab_ref, out_ref):
    size, width = slab_ref.shape[1:]
    row = lax.broadcasted_iota(jnp.int32, (size, width), 0) + pl.program_id(0) * size
    here = lax.broadcasted_iota(jnp.int32, (size, width), 1) == row
    total = jnp.zeros(out_ref.shape, f32)
    for p in range(vectors_ref.shape[0]):
        diagonal = jnp.sum(jnp.where(here, slab_ref[p], 0.0), axis=1, keepdims=True)
        total = total + vectors_ref[p] * diagonal
    out_ref[...] = total


def gradient_terms(chol_vectors, me):
    vectors, rows, orbitals = chol_vectors.shape
    size = 16
    return pl.pallas_call(
        gradient_kernel,
        grid_spec=pltpu.PrefetchScalarGridSpec(
            num_scalar_prefetch=1,
            grid=(rows // size,),
            in_specs=[
                pl.BlockSpec((vectors, size, orbitals), lambda i, me: (0, i, 0)),
                pl.BlockSpec((vectors, size, rows), lambda i, me: (0, i, me[0])),
            ],
            out_specs=pl.BlockSpec((size, orbitals), lambda i, me: (i, 0)),
        ),
        out_shape=jax.ShapeDtypeStruct((rows, orbitals), f32),
        cost_estimate=cost(2 * chol_vectors.size, 4 * chol_vectors.size),
        name="gradient_terms",
    )(me, chol_vectors, chol_vectors)


def skew_part(terms_ref, sign, skew_ref, upper_ref, lower_ref):
    def body(i, total):
        at = pl.ds(pl.multiple_of(i * lane, lane), lane)
        skew = sign * (terms_ref[at, :] - terms_ref[:, at].T)
        skew_ref[at, :] = skew
        upper_ref[at, :], lower_ref[at, :] = split(skew)
        return total + jnp.sum(skew * skew, axis=(0, 1), keepdims=True)

    return lax.fori_loop(0, skew_ref.shape[0] // lane, body, jnp.zeros((1, 1), f32))


def step_parts(total, skew_ref, upper_ref, lower_ref, store):
    orbitals = skew_ref.shape[0]
    norm = jnp.sqrt(total / (orbitals * orbitals) + 1e-06)
    scale = step_gain / jnp.sqrt(jnp.full((1, 1), orbitals, f32)) / norm
    tile = orbitals // 2

    @pl.loop(0, 2)
    def _(t):
        at = pl.ds(pl.multiple_of(t * tile, tile), tile)
        square = product(
            (upper_ref[at, :], lower_ref[at, :]), (upper_ref[...], lower_ref[...])
        )
        row = lax.broadcasted_iota(jnp.int32, (tile, orbitals), 0) + t * tile
        column = lax.broadcasted_iota(jnp.int32, (tile, orbitals), 1)
        even = jnp.where(row == column, 1.0, 0.0) + (0.5 * scale * scale) * square
        store(at, even, scale * skew_ref[at, :])


def first_kernel(devices, me_ref, *refs):
    shards, refs = refs[:devices], refs[devices:]
    step, turned = refs[:2], refs[2:4]
    terms, skew, upper, lower = refs[4:]
    rows = shards[0].shape[0]
    for k in range(devices):
        terms[pl.ds(pl.multiple_of((me_ref[0] ^ k) * rows, rows), rows), :] = shards[k][...]
    total = skew_part(terms, 1.0, skew, upper, lower)

    def store(at, even, odd):
        step[0][at, :], step[1][at, :] = split(even + odd)
        turned[0][at, :], turned[1][at, :] = split(even - odd)

    step_parts(total, skew, upper, lower, store)


def second_kernel(devices, me_ref, *refs):
    shards, turned, refs = refs[:devices], refs[devices : devices + 2], refs[devices + 2 :]
    step, ordered = refs[:2], refs[2:4]
    terms, skew, upper, lower = refs[4:]
    rows = shards[0].shape[0]
    orbitals = terms.shape[0]
    me = me_ref[0]
    for k in range(devices):
        at = pl.ds(pl.multiple_of((me ^ k) * rows, rows), rows)
        upper[at, :], lower[at, :] = split(shards[k][...])
    tile = orbitals // 2

    @pl.loop(0, 2)
    def _(t):
        at = pl.ds(pl.multiple_of(t * tile, tile), tile)
        terms[at, :] = product(
            (turned[0][at, :], turned[1][at, :]), (upper[...], lower[...])
        )

    total = skew_part(terms, -1.0, skew, upper, lower)

    def store(at, even, odd):
        whole = even + odd
        step[0][at, :], step[1][at, :] = split(whole)
        terms[at, :] = whole
        for k in range(devices):
            source = pl.ds(pl.multiple_of((me ^ k) * rows, rows), rows)
            here = pl.ds(k * rows, rows)
            ordered[0][at, here], ordered[1][at, here] = split(terms[at, source])

    step_parts(total, skew, upper, lower, store)


def make_step(kernel, me, shards, extra):
    devices = len(shards)
    orbitals = shards[0].shape[1]
    square = (orbitals, orbitals)
    part = jax.ShapeDtypeStruct(square, bf16)
    return pl.pallas_call(
        functools.partial(kernel, devices),
        in_specs=[pl.BlockSpec(memory_space=pltpu.SMEM)]
        + [whole_spec()] * (devices + len(extra)),
        out_specs=[whole_spec()] * 4,
        out_shape=[part] * 4,
        scratch_shapes=[
            pltpu.VMEM(square, f32),
            pltpu.VMEM(square, f32),
            pltpu.VMEM(square, bf16),
            pltpu.VMEM(square, bf16),
        ],
        cost_estimate=cost(12 * orbitals**3, 24 * orbitals**2),
    )(me, *shards, *extra)


def compose_kernel(devices, me_ref, left_upper, left_lower, right_upper, right_lower, *refs):
    by_column, by_row, own_ref, whole = refs[:2], refs[2:4], refs[4], refs[5]
    rows = own_ref.shape[0]
    tile = whole.shape[0] // 2
    me = me_ref[0]

    @pl.loop(0, 2)
    def _(t):
        at = pl.ds(pl.multiple_of(t * tile, tile), tile)
        whole[at, :] = product(
            (left_upper[at, :], left_lower[at, :]), (right_upper[...], right_lower[...])
        )

    own_ref[...] = whole[pl.ds(pl.multiple_of(me * rows, rows), rows), :]
    for k in range(devices):
        source = pl.ds(pl.multiple_of((me ^ k) * rows, rows), rows)
        here = pl.ds(k * rows, rows)
        by_column[0][:, here], by_column[1][:, here] = split(whole[:, source])
        by_row[0][here, :], by_row[1][here, :] = split(whole[source, :])


def compose(me, left, right, devices):
    orbitals = left[0].shape[0]
    square = (orbitals, orbitals)
    part = jax.ShapeDtypeStruct(square, bf16)
    out = pl.pallas_call(
        functools.partial(compose_kernel, devices),
        in_specs=[pl.BlockSpec(memory_space=pltpu.SMEM)] + [whole_spec()] * 4,
        out_specs=[whole_spec()] * 5,
        out_shape=[part] * 4 + [jax.ShapeDtypeStruct((orbitals // devices, orbitals), f32)],
        scratch_shapes=[pltpu.VMEM(square, f32)],
        cost_estimate=cost(6 * orbitals**3, 16 * orbitals**2),
        name="compose",
    )(me, *left, *right)
    return out[:2], out[2:4], out[4]


def first_product_kernel(vectors_ref, upper, lower, rows_upper, rows_lower, out_upper, out_lower, diagonal):
    size, rows, orbitals = vectors_ref.shape
    own = rows_upper[...].astype(f32) + rows_lower[...].astype(f32)
    for q in range(0, size, quad):
        at = pl.ds(q, quad)
        vectors = vectors_ref[at].reshape(quad * rows, orbitals)
        left = product(split(vectors), (upper[...], lower[...])).reshape(quad, rows, orbitals)
        out_upper[at], out_lower[at] = split(left)
        diagonal[at] = jnp.sum(left * own[None], axis=1)


def first_product(chol_vectors, step, me):
    vectors, rows, orbitals = chol_vectors.shape
    size = 2 * quad
    part = jax.ShapeDtypeStruct(chol_vectors.shape, bf16)
    block = pl.BlockSpec((size, rows, orbitals), lambda i, me: (i, 0, 0))
    square = pl.BlockSpec(
        (orbitals, orbitals), lambda i, me: (0, 0), pipeline_mode=pl.Buffered(1)
    )
    own = pl.BlockSpec((rows, orbitals), lambda i, me: (me[0], 0))
    out = pl.pallas_call(
        lambda me_ref, *refs: first_product_kernel(*refs),
        grid_spec=pltpu.PrefetchScalarGridSpec(
            num_scalar_prefetch=1,
            grid=(vectors // size,),
            in_specs=[block, square, square, own, own],
            out_specs=[block, block, pl.BlockSpec((size, orbitals), lambda i, me: (i, 0))],
        ),
        out_shape=[part, part, jax.ShapeDtypeStruct((vectors, orbitals), f32)],
        cost_estimate=cost(6 * chol_vectors.size * orbitals, 8 * chol_vectors.size),
        name="first_product",
    )(me, chol_vectors, *step, *step)
    return out[:2], out[2]


def pieces_kernel(rows, left_upper, left_lower, upper, lower, *outs):
    count = left_upper.shape[0]
    left = tuple(r[...].reshape(count * rows, -1) for r in (left_upper, left_lower))
    value = product(left, (upper[...], lower[...]))
    for k, out in enumerate(outs):
        for p in range(count):
            out[p] = value[p * rows : (p + 1) * rows, k * rows : (k + 1) * rows].T


def plain_pieces(lefts, right, vectors, devices):
    rows, orbitals = lefts[0].shape[1:]
    block = pl.BlockSpec((quad, rows, orbitals), lambda i: (i, 0, 0))
    return pl.pallas_call(
        functools.partial(pieces_kernel, rows),
        grid=(vectors // quad,),
        in_specs=[block] * 2 + [resident((orbitals, orbitals))] * 2,
        out_specs=[pl.BlockSpec((quad, rows, rows), lambda i: (i, 0, 0))] * devices,
        out_shape=[jax.ShapeDtypeStruct((vectors, rows, rows), f32)] * devices,
        cost_estimate=cost(6 * vectors * rows * orbitals**2, 8 * vectors * rows * orbitals),
        name="plain_pieces",
    )(*lefts, *right)


def turns(side):
    return (lambda i: jnp.minimum(i, 1)) if side == 0 else (lambda i: jnp.maximum(i - 2, 0))


def shared_pieces_kernel(near, rows, own, one, two, upper, lower, *outs):
    count = own.shape[0]
    half = len(outs) // 2
    for side, other in enumerate((one, two)):
        @pl.when(pl.program_id(0) // 2 == side)
        def _():
            right = tuple(
                jnp.concatenate([r[:, k * rows : (k + 1) * rows] for k in near[side]], axis=1)
                for r in (upper, lower)
            )
            left = jnp.concatenate([own[...], other[...]], axis=0)
            value = product(split(left.reshape(2 * count * rows, -1)), right)
            for b in range(half):
                for p in range(2 * count):
                    block = value[p * rows : (p + 1) * rows, b * rows : (b + 1) * rows]
                    outs[side * half + b][p % count, p // count] = block.T


def shared_pieces(near, chol_vectors, starts, others, right):
    _, rows, orbitals = chol_vectors.shape
    half = len(near[0])
    first, second = (start // 2 for start in starts)
    specs = [
        pl.BlockSpec(
            (2, rows, orbitals), lambda i: (jnp.where(i < 2, first + i, second + i - 2), 0, 0)
        )
    ]
    outs = []
    for side in range(2):
        turn_of = turns(side)
        specs.append(pl.BlockSpec((2, rows, orbitals), lambda i, t=turn_of: (t(i), 0, 0)))
        outs += [
            pl.BlockSpec((2, 2, rows, rows), lambda i, t=turn_of: (t(i), 0, 0, 0))
        ] * half
    out = pl.pallas_call(
        functools.partial(shared_pieces_kernel, near, rows),
        grid=(4,),
        in_specs=specs + [resident((orbitals, orbitals))] * 2,
        out_specs=outs,
        out_shape=[jax.ShapeDtypeStruct((quad, 2, rows, rows), f32)] * (2 * half),
        cost_estimate=cost(
            12 * quad * rows * orbitals**2, 16 * quad * rows * orbitals
        ),
        name="shared_pieces",
    )(chol_vectors, *others, *right)
    return out[:half], out[half:]


def rotated_kernel(upper, lower, *refs):
    parts, out_ref = refs[:-1], refs[-1]
    count, rows, _ = out_ref.shape
    left = jnp.concatenate([r[...].reshape(count * rows, rows) for r in parts], axis=1)
    out_ref[...] = product(split(left), (upper[...], lower[...])).reshape(out_ref.shape)


def plain_rotated(shape, parts, right):
    vectors, rows = parts[0].shape[:2]
    orbitals = shape[2]
    part = pl.BlockSpec((quad, rows, rows), lambda i: (i, 0, 0))
    return pl.pallas_call(
        rotated_kernel,
        grid=(vectors // quad,),
        in_specs=[resident((orbitals, orbitals))] * 2
        + [part] * len(parts),
        out_specs=pl.BlockSpec((quad, rows, orbitals), lambda i: (i, 0, 0)),
        out_shape=jax.ShapeDtypeStruct(shape, f32),
        cost_estimate=cost(6 * vectors * rows * orbitals**2, 8 * vectors * rows * orbitals),
        name="plain_rotated",
    )(*right, *parts)


def shared_rotated_kernel(orders, upper, lower, *refs):
    out_ref = refs[-1]
    count, rows, _ = out_ref.shape
    half = len(orders[0]) // 2
    for side, order in enumerate(orders):
        @pl.when(pl.program_id(0) // 2 == side)
        def _():
            columns = [
                refs[side * half + index][:, which].reshape(count * rows, rows)
                for index, which in order
            ]
            left = split(jnp.concatenate(columns, axis=1))
            out_ref[...] = product(left, (upper[...], lower[...])).reshape(out_ref.shape)


def shared_rotated(previous, parts, orders, starts, right, shape):
    _, rows, orbitals = shape
    fresh = previous is None
    first, second = (start // 2 for start in starts)
    specs = []
    for side in range(2):
        turn_of = turns(side)
        specs += [
            pl.BlockSpec((2, 2, rows, rows), lambda i, t=turn_of: (t(i), 0, 0, 0))
        ] * len(parts[side])
    count = 2 + len(specs)
    return pl.pallas_call(
        functools.partial(shared_rotated_kernel, orders),
        grid=(4,),
        in_specs=[resident((orbitals, orbitals))] * 2
        + specs
        + ([] if fresh else [pl.BlockSpec(memory_space=pl.ANY)]),
        out_specs=pl.BlockSpec(
            (2, rows, orbitals), lambda i: (jnp.where(i < 2, first + i, second + i - 2), 0, 0)
        ),
        out_shape=jax.ShapeDtypeStruct(shape, f32),
        input_output_aliases={} if fresh else {count: 0},
        cost_estimate=cost(12 * quad * rows * orbitals**2, 16 * quad * rows * orbitals),
        name="shared_rotated",
    )(*right, *parts[0], *parts[1], *([] if fresh else [previous]))


def second_terms_kernel(upper_ref, lower_ref, diagonal_ref, out_ref):
    total = jnp.zeros(out_ref.shape, f32)
    for p in range(upper_ref.shape[0]):
        left = upper_ref[p].astype(f32) + lower_ref[p].astype(f32)
        total = total + left * diagonal_ref[p : p + 1, :]
    out_ref[...] = total


def second_terms(lefts, diagonal):
    vectors, rows, orbitals = lefts[0].shape
    size = 16
    block = pl.BlockSpec((vectors, size, orbitals), lambda i: (0, i, 0))
    return pl.pallas_call(
        second_terms_kernel,
        grid=(rows // size,),
        in_specs=[block, block, pl.BlockSpec((vectors, orbitals), lambda i: (0, 0))],
        out_specs=pl.BlockSpec((size, orbitals), lambda i: (i, 0)),
        out_shape=jax.ShapeDtypeStruct((rows, orbitals), f32),
        cost_estimate=cost(2 * lefts[0].size, 4 * lefts[0].size),
        name="second_terms",
    )(*lefts, diagonal)


def flip(x, k):
    count = lax.axis_size("vec")
    return lax.ppermute(x, "vec", [(i, i ^ k) for i in range(count)])


def sum_halves(part):
    bits = lax.axis_size("vec").bit_length() - 1
    masks = [2 ** (b + 1) - 1 for b in range(bits)]
    half = part.shape[0] // 2
    one, two = part[:half], part[half:]
    for a, b in zip(masks, reversed(masks)):
        one, two = one + flip(one, a), two + flip(two, b)
    return jnp.concatenate([one, two], axis=0)


def shards_of(part):
    out = []
    for k in range(0, lax.axis_size("row"), 2):
        mine = part if k == 0 else swap(part, k)
        out += [mine, swap(mine, 1)]
    return out


def after(x, *others):
    return lax.optimization_barrier((x,) + others)[0]


def tiled_shards(chol_vectors):
    shape = chol_vectors.shape
    vectors, _, _ = shape
    devices = lax.axis_size("row")
    me = lax.axis_index("row").astype(jnp.int32)[None]
    groups = shared_groups(vectors)
    plain = vectors - 2 * quad * groups
    bits = (devices // 2, devices // 4)
    everyone = list(range(devices))
    near = [[k for k in everyone if not k & bit] for bit in bits]
    orders = [
        [(near[s].index(k & ~bit), int(bool(k & bit))) for k in everyone]
        for s, bit in enumerate(bits)
    ]
    starts = [
        [plain + (s * groups + g) * quad for s in range(2)] for g in range(groups)
    ]

    own = [[chol_vectors[start : start + quad] for start in starts[g]] for g in range(groups)]
    early = {}

    def send_early(g, *others):
        for s, bit in enumerate(bits):
            early[g, s] = swap(after(own[g][s], *others), bit)

    part = gradient_terms(chol_vectors, me)
    part = sum_halves(part)
    gathered = shards_of(part)
    for g in range(groups - 1):
        send_early(g, *gathered)
    *step, turned_upper, turned_lower = make_step(first_kernel, me, gathered, ())
    lefts, diagonal = first_product(chol_vectors, step, me)
    diagonal = sum_over_row(diagonal)
    part = second_terms(lefts, diagonal)
    gathered = shards_of(sum_halves(part))
    send_early(groups - 1, *gathered)
    *next_step, ordered_upper, ordered_lower = make_step(
        second_kernel, me, gathered, (turned_upper, turned_lower)
    )
    sent = plain_pieces(lefts, (ordered_upper, ordered_lower), plain, devices)
    plain_parts = [sent[0]] + [swap(sent[k], k) for k in everyone[1:]]
    next_step = lax.optimization_barrier((*next_step, *sent))[:2]
    by_column, by_row, rotation = compose(me, step, next_step, devices)

    shared_parts = []
    for g in range(groups):
        others = (early[g, 0], early[g, 1])
        sent = shared_pieces(near, chol_vectors, starts[g], others, by_column)
        shared_parts.append(
            [
                [pieces[0]] + [swap(pieces[i], near[s][i]) for i in range(1, len(near[s]))]
                for s, pieces in enumerate(sent)
            ]
        )
        by_column = lax.optimization_barrier((*by_column, *sent[0], *sent[1]))[:2]
    rotated = plain_rotated(shape, plain_parts, by_row)
    for g in range(groups):
        rotated = shared_rotated(rotated, shared_parts[g], orders, starts[g], by_row, shape)
    return rotated, rotation


def shared_groups(vectors):
    return (3 * vectors // 4) // (2 * quad)


def shards(chol_vectors):
    vectors, rows, _ = chol_vectors.shape
    devices, groups = lax.axis_size("row"), lax.axis_size("vec")
    tiled = rows % lane == 0 and vectors % (2 * quad) == 0 and devices >= 8
    if tiled and devices & (devices - 1) == 0 and groups & (groups - 1) == 0:
        return tiled_shards(chol_vectors)
    return plain_shards(chol_vectors)


def solution(mesh):
    return jax.shard_map(
        shards,
        mesh=mesh,
        in_specs=(P("vec", "row", None),),
        out_specs=(P("vec", "row", None), P("row", None)),
        check_vma=False,
    )
```

```python
import functools

import jax
import jax.numpy as jnp
from jax import lax
from jax.experimental import pallas as pl
from jax.experimental.pallas import tpu as pltpu
from jax.sharding import PartitionSpec as P


step_gain = 0.2
chunk_count = 4
high = lax.Precision.HIGH


def swap(x, k):
    count = lax.axis_size("row")
    return lax.ppermute(x, "row", [(i, i ^ k) for i in range(count)])


def turn(x, k):
    count = lax.axis_size("vec")
    return lax.ppermute(x, "vec", [(i, (i + k) % count) for i in range(count)])


def cut(x, index, size, axis):
    return lax.dynamic_slice_in_dim(x, index * size, size, axis)


def place(whole, part, index):
    return lax.dynamic_update_slice_in_dim(whole, part, index * part.shape[0], 0)


def sum_over_vec(part):
    count = lax.axis_size("vec")
    me = lax.axis_index("vec")
    size = part.shape[0] // count
    total = cut(part, me, size, 0)
    for k in range(1, count):
        total = total + turn(cut(part, (me + k) % count, size, 0), k)
    whole = place(jnp.zeros_like(part), total, me)
    for k in range(1, count):
        whole = place(whole, turn(total, k), (me - k) % count)
    return whole


def gather_rows(part):
    count = lax.axis_size("row")
    me = lax.axis_index("row")
    whole = jnp.zeros((count * part.shape[0], part.shape[1]), part.dtype)
    for k in range(0, count, 2):
        mine = part if k == 0 else swap(part, k)
        whole = place(whole, mine, me ^ k)
        whole = place(whole, swap(mine, 1), me ^ k ^ 1)
    return whole


def sum_over_row(part):
    pair = part + swap(part, 1)
    total = pair
    for k in range(2, lax.axis_size("row"), 2):
        total = total + swap(pair, k)
    return total


def step_of(gradient):
    orbitals = gradient.shape[0]
    norm = jnp.sqrt(jnp.sum(gradient * gradient) / (orbitals * orbitals) + 1e-06)
    generator = step_gain / jnp.sqrt(jnp.float32(orbitals)) * gradient / norm
    square = jnp.dot(generator, generator, precision=high)
    return jnp.eye(orbitals, dtype=jnp.float32) + generator + 0.5 * square


def plain_shards(chol_vectors):
    vectors, rows, orbitals = chol_vectors.shape
    devices = lax.axis_size("row")
    me = lax.axis_index("row")
    chunk = vectors // chunk_count

    block = cut(chol_vectors, me, rows, 2)
    here = jnp.eye(rows, dtype=jnp.bool_)
    diagonal = jnp.sum(jnp.where(here, block, 0.0), axis=2)
    part = jnp.sum(chol_vectors * diagonal[:, :, None], axis=0)
    terms = gather_rows(sum_over_vec(part))
    step = step_of(terms - terms.T)

    step_rows = cut(step, me, rows, 0)
    lefts = []
    part = jnp.zeros((rows, orbitals), jnp.float32)
    for c in range(chunk_count):
        own = chol_vectors[c * chunk : (c + 1) * chunk]
        left = jnp.einsum("pab,bm->pam", own, step, precision=high)
        lefts.append(left)
        diagonal = sum_over_row(jnp.sum(left * step_rows, axis=1))
        part = part + jnp.sum(left * diagonal[:, None, :], axis=0)
    terms = gather_rows(sum_over_vec(part))
    terms = lax.dot_general(step, terms, (((0,), (0,)), ((), ())), precision=high)
    step_next = step_of(terms.T - terms)
    rotation = jnp.dot(step, step_next, precision=high)
    order = me ^ jnp.arange(devices)
    rotation_order = rotation.reshape(devices, rows, orbitals)[order].reshape(orbitals, orbitals)

    outs = []
    for c in range(chunk_count):
        left = jnp.einsum("pab,bm->pam", lefts[c], step_next, precision=high)
        pieces = []
        for k in range(devices):
            piece = cut(left, me ^ k, rows, 2)
            pieces.append(piece if k == 0 else swap(piece, k))
        columns = jnp.concatenate(pieces, axis=1)
        outs.append(jnp.einsum("pam,ak->pmk", columns, rotation_order, precision=high))
    return jnp.concatenate(outs, axis=0), cut(rotation, me, rows, 0)


lane = 128
band = 256
room = pltpu.CompilerParams(vmem_limit_bytes=28 << 20)
quad = 4
bf16, f32 = jnp.bfloat16, jnp.float32


def split(x):
    upper = x.astype(bf16)
    return upper, (x - upper.astype(f32)).astype(bf16)


def product(left, right):
    dot = functools.partial(jnp.dot, preferred_element_type=f32)
    return dot(left[0], right[0]) + (dot(left[0], right[1]) + dot(left[1], right[0]))


def whole_spec():
    return pl.BlockSpec(memory_space=pltpu.VMEM)


def resident(shape):
    return pl.BlockSpec(shape, lambda i: (0,) * len(shape), pipeline_mode=pl.Buffered(1))


def cost(flops, data):
    return pl.CostEstimate(flops=flops, bytes_accessed=data, transcendentals=0)


def gradient_kernel(me_ref, vectors_ref, slab_ref, out_ref):
    size, width = slab_ref.shape[1:]
    row = lax.broadcasted_iota(jnp.int32, (size, width), 0) + pl.program_id(0) * size
    here = lax.broadcasted_iota(jnp.int32, (size, width), 1) == row
    total = jnp.zeros(out_ref.shape, f32)
    for p in range(vectors_ref.shape[0]):
        diagonal = jnp.sum(jnp.where(here, slab_ref[p], 0.0), axis=1, keepdims=True)
        total = total + vectors_ref[p] * diagonal
    out_ref[...] = total


def gradient_terms(chol_vectors, me):
    vectors, rows, orbitals = chol_vectors.shape
    size = 16
    return pl.pallas_call(
        gradient_kernel,
        grid_spec=pltpu.PrefetchScalarGridSpec(
            num_scalar_prefetch=1,
            grid=(rows // size,),
            in_specs=[
                pl.BlockSpec((vectors, size, orbitals), lambda i, me: (0, i, 0)),
                pl.BlockSpec((vectors, size, rows), lambda i, me: (0, i, me[0])),
            ],
            out_specs=pl.BlockSpec((size, orbitals), lambda i, me: (i, 0)),
        ),
        out_shape=jax.ShapeDtypeStruct((rows, orbitals), f32),
        cost_estimate=cost(2 * chol_vectors.size, 4 * chol_vectors.size),
        compiler_params=room,
        name="gradient_terms",
    )(me, chol_vectors, chol_vectors)


def skew_part(terms_ref, sign, skew_ref, upper_ref, lower_ref):
    def body(i, total):
        at = pl.ds(pl.multiple_of(i * lane, lane), lane)
        skew = sign * (terms_ref[at, :] - terms_ref[:, at].T)
        skew_ref[at, :] = skew
        upper_ref[at, :], lower_ref[at, :] = split(skew)
        return total + jnp.sum(skew * skew, axis=(0, 1), keepdims=True)

    return lax.fori_loop(0, skew_ref.shape[0] // lane, body, jnp.zeros((1, 1), f32))


def columns_of(t, width):
    return pl.ds(pl.multiple_of(t * width, width), width)


def step_parts(total, skew_ref, upper_ref, lower_ref, store):
    orbitals = skew_ref.shape[0]
    norm = jnp.sqrt(total / (orbitals * orbitals) + 1e-06)
    scale = step_gain / jnp.sqrt(jnp.full((1, 1), orbitals, f32)) / norm

    @pl.loop(0, orbitals // band)
    def _(t):
        at = columns_of(t, band)
        square = product(
            (upper_ref[...], lower_ref[...]), (upper_ref[:, at], lower_ref[:, at])
        )
        row = lax.broadcasted_iota(jnp.int32, (orbitals, band), 0)
        column = lax.broadcasted_iota(jnp.int32, (orbitals, band), 1) + t * band
        even = jnp.where(row == column, 1.0, 0.0) + (0.5 * scale * scale) * square
        store(t, at, even, scale * skew_ref[:, at])


def first_kernel(devices, me_ref, *refs):
    shards, refs = refs[:devices], refs[devices:]
    step, turned = refs[:2], refs[2:4]
    terms, skew, upper, lower = refs[4:]
    rows = shards[0].shape[0]
    for k in range(devices):
        terms[pl.ds(pl.multiple_of((me_ref[0] ^ k) * rows, rows), rows), :] = shards[k][...]
    total = skew_part(terms, 1.0, skew, upper, lower)

    def store(t, at, even, odd):
        step[0][:, at], step[1][:, at] = split(even + odd)
        turned[0][:, at], turned[1][:, at] = split(even - odd)

    step_parts(total, skew, upper, lower, store)


def second_kernel(devices, me_ref, *refs):
    shards, turned, refs = refs[:devices], refs[devices : devices + 2], refs[devices + 2 :]
    ordered, (terms, skew, upper, lower) = refs[:2], refs[2:]
    rows = shards[0].shape[0]
    orbitals = terms.shape[0]
    me = me_ref[0]
    for k in range(devices):
        at = pl.ds(pl.multiple_of((me ^ k) * rows, rows), rows)
        upper[at, :], lower[at, :] = split(shards[k][...])

    @pl.loop(0, orbitals // band)
    def _(t):
        at = columns_of(t, band)
        terms[:, at] = product(
            (turned[0][...], turned[1][...]), (upper[:, at], lower[:, at])
        )

    total = skew_part(terms, -1.0, skew, upper, lower)

    def store(t, at, even, odd):
        whole = even + odd
        for b in range(band // rows):
            column = t * (band // rows) + b
            here = pl.ds(pl.multiple_of((me ^ column) * rows, rows), rows)
            part = whole[:, b * rows : (b + 1) * rows]
            ordered[0][:, here], ordered[1][:, here] = split(part)

    step_parts(total, skew, upper, lower, store)


def make_step(kernel, me, shards, extra, count):
    devices = len(shards)
    orbitals = shards[0].shape[1]
    square = (orbitals, orbitals)
    part = jax.ShapeDtypeStruct(square, bf16)
    return pl.pallas_call(
        functools.partial(kernel, devices),
        in_specs=[pl.BlockSpec(memory_space=pltpu.SMEM)]
        + [whole_spec()] * (devices + len(extra)),
        out_specs=[whole_spec()] * count,
        out_shape=[part] * count,
        scratch_shapes=[
            pltpu.VMEM(square, f32),
            pltpu.VMEM(square, f32),
            pltpu.VMEM(square, bf16),
            pltpu.VMEM(square, bf16),
        ],
        cost_estimate=cost(12 * orbitals**3, 24 * orbitals**2),
        compiler_params=room,
    )(me, *shards, *extra)


def compose_kernel(devices, me_ref, left_upper, left_lower, right_upper, right_lower, *refs):
    by_column, by_row, own_ref, whole = refs[:2], refs[2:4], refs[4], refs[5]
    rows = own_ref.shape[0]
    orbitals = whole.shape[0]
    me = me_ref[0]

    @pl.loop(0, orbitals // band)
    def _(t):
        at = columns_of(t, band)
        value = product(
            (left_upper[...], left_lower[...]), (right_upper[:, at], right_lower[:, at])
        )
        by_column[0][:, at], by_column[1][:, at] = split(value)
        for b in range(band // rows):
            column = t * (band // rows) + b
            here = pl.ds(pl.multiple_of((me ^ column) * rows, rows), rows)
            whole[:, here] = value[:, b * rows : (b + 1) * rows]

    own_ref[...] = whole[pl.ds(pl.multiple_of(me * rows, rows), rows), :]
    for k in range(devices):
        source = pl.ds(pl.multiple_of((me ^ k) * rows, rows), rows)
        here = pl.ds(k * rows, rows)
        by_row[0][here, :], by_row[1][here, :] = split(whole[source, :])


def compose(me, left, right, devices):
    orbitals = left[0].shape[0]
    square = (orbitals, orbitals)
    part = jax.ShapeDtypeStruct(square, bf16)
    out = pl.pallas_call(
        functools.partial(compose_kernel, devices),
        in_specs=[pl.BlockSpec(memory_space=pltpu.SMEM)] + [whole_spec()] * 4,
        out_specs=[whole_spec()] * 5,
        out_shape=[part] * 4 + [jax.ShapeDtypeStruct((orbitals // devices, orbitals), f32)],
        scratch_shapes=[pltpu.VMEM(square, f32)],
        cost_estimate=cost(6 * orbitals**3, 16 * orbitals**2),
        compiler_params=room,
        name="compose",
    )(me, *left, *right)
    return out[:2], out[2:4], out[4]


def first_product_kernel(me_ref, vectors_ref, upper, lower, rows_upper, rows_lower, out_upper, out_lower, diagonal):
    size, rows, orbitals = vectors_ref.shape
    own = rows_upper[...].astype(f32) + rows_lower[...].astype(f32)
    vectors = vectors_ref[...].reshape(size * rows, orbitals)
    left = product(split(vectors), (upper[...], lower[...])).reshape(size, rows, orbitals)
    out_upper[...], out_lower[...] = split(left)
    diagonal[...] = jnp.sum(left * own[None], axis=1, keepdims=True)


def first_product(chol_vectors, step, me):
    vectors, rows, orbitals = chol_vectors.shape
    part = jax.ShapeDtypeStruct(chol_vectors.shape, bf16)
    block = pl.BlockSpec((quad, rows, orbitals), lambda i, me: (i, 0, 0))
    square = pl.BlockSpec(
        (orbitals, orbitals), lambda i, me: (0, 0), pipeline_mode=pl.Buffered(1)
    )
    own = pl.BlockSpec((rows, orbitals), lambda i, me: (me[0], 0))
    out = pl.pallas_call(
        first_product_kernel,
        grid_spec=pltpu.PrefetchScalarGridSpec(
            num_scalar_prefetch=1,
            grid=(vectors // quad,),
            in_specs=[block, square, square, own, own],
            out_specs=[block, block, pl.BlockSpec((quad, 1, orbitals), lambda i, me: (i, 0, 0))],
        ),
        out_shape=[part, part, jax.ShapeDtypeStruct((vectors, 1, orbitals), f32)],
        cost_estimate=cost(6 * chol_vectors.size * orbitals, 8 * chol_vectors.size),
        compiler_params=room,
        name="first_product",
    )(me, chol_vectors, *step, *step)
    return out[:2], out[2]


def pieces_kernel(rows, left_upper, left_lower, upper, lower, *outs):
    count = left_upper.shape[0]
    left = tuple(r[...].reshape(count * rows, -1) for r in (left_upper, left_lower))
    value = product(left, (upper[...], lower[...]))
    for k, out in enumerate(outs):
        for p in range(count):
            out[p] = value[p * rows : (p + 1) * rows, k * rows : (k + 1) * rows].T


def plain_pieces(lefts, right, vectors, devices):
    rows, orbitals = lefts[0].shape[1:]
    block = pl.BlockSpec((quad, rows, orbitals), lambda i: (i, 0, 0))
    return pl.pallas_call(
        functools.partial(pieces_kernel, rows),
        grid=(vectors // quad,),
        in_specs=[block] * 2 + [resident((orbitals, orbitals))] * 2,
        out_specs=[pl.BlockSpec((quad, rows, rows), lambda i: (i, 0, 0))] * devices,
        out_shape=[jax.ShapeDtypeStruct((vectors, rows, rows), f32)] * devices,
        cost_estimate=cost(6 * vectors * rows * orbitals**2, 8 * vectors * rows * orbitals),
        compiler_params=room,
        name="plain_pieces",
    )(*lefts, *right)


def turns(side):
    return (lambda i: jnp.minimum(i, 1)) if side == 0 else (lambda i: jnp.maximum(i - 2, 0))


def shared_pieces_kernel(pair, own, *refs):
    others, (upper, lower), refs = refs[:4], refs[4:6], refs[6:]
    outs, (left_upper, left_lower, blocks) = refs[:-3], refs[-3:]
    count, rows, orbitals = own.shape
    half = len(outs) // 2
    step = pl.program_id(0)
    size = count * rows
    left_upper[:size], left_lower[:size] = split(own[...].reshape(size, orbitals))
    for i, other in enumerate(others):
        @pl.when(step == i)
        def _():
            left_upper[size:], left_lower[size:] = split(other[...].reshape(size, orbitals))

    left = left_upper[...], left_lower[...]
    middle = pl.ds(pl.multiple_of((1 + step // 2) * pair, pair), pair)
    for n, at in enumerate((pl.ds(0, pair), middle)):
        value = product(left, (upper[:, at], lower[:, at]))
        for b in range(half // 2):
            for p in range(2 * count):
                block = value[p * rows : (p + 1) * rows, b * rows : (b + 1) * rows]
                blocks[n * (half // 2) + b, p % count, p // count] = block.T
    for side in range(2):
        @pl.when(step // 2 == side)
        def _():
            for b in range(half):
                outs[side * half + b][...] = blocks[b]


def shared_pieces(near, chol_vectors, starts, others, right):
    _, rows, orbitals = chol_vectors.shape
    half = len(near[0])
    first, second = (start // 2 for start in starts)
    specs = [
        pl.BlockSpec(
            (2, rows, orbitals), lambda i: (jnp.where(i < 2, first + i, second + i - 2), 0, 0)
        )
    ] + [resident((2, rows, orbitals))] * 4
    outs = []
    for side in range(2):
        turn_of = turns(side)
        outs += [
            pl.BlockSpec((2, 2, rows, rows), lambda i, t=turn_of: (t(i), 0, 0, 0))
        ] * half
    out = pl.pallas_call(
        functools.partial(shared_pieces_kernel, orbitals // 4),
        grid=(4,),
        in_specs=specs + [resident((orbitals, orbitals))] * 2,
        out_specs=outs,
        out_shape=[jax.ShapeDtypeStruct((quad, 2, rows, rows), f32)] * (2 * half),
        scratch_shapes=[
            pltpu.VMEM((4 * rows, orbitals), bf16),
            pltpu.VMEM((4 * rows, orbitals), bf16),
            pltpu.VMEM((half, 2, 2, rows, rows), f32),
        ],
        cost_estimate=cost(
            12 * quad * rows * orbitals**2, 16 * quad * rows * orbitals
        ),
        compiler_params=room,
        name="shared_pieces",
    )(chol_vectors, *others, *right)
    return out[:half], out[half:]


def rotated_kernel(upper, lower, *refs):
    parts, out_ref = refs[:-1], refs[-1]
    count, rows, _ = out_ref.shape
    left = jnp.concatenate([r[...].reshape(count * rows, rows) for r in parts], axis=1)
    out_ref[...] = product(split(left), (upper[...], lower[...])).reshape(out_ref.shape)


def plain_rotated(shape, parts, right):
    vectors, rows = parts[0].shape[:2]
    orbitals = shape[2]
    part = pl.BlockSpec((quad, rows, rows), lambda i: (i, 0, 0))
    return pl.pallas_call(
        rotated_kernel,
        grid=(vectors // quad,),
        in_specs=[resident((orbitals, orbitals))] * 2
        + [part] * len(parts),
        out_specs=pl.BlockSpec((quad, rows, orbitals), lambda i: (i, 0, 0)),
        out_shape=jax.ShapeDtypeStruct(shape, f32),
        cost_estimate=cost(6 * vectors * rows * orbitals**2, 8 * vectors * rows * orbitals),
        compiler_params=room,
        name="plain_rotated",
    )(*right, *parts)


def shared_rotated_kernel(orders, upper, lower, *refs):
    out_ref, left_upper, left_lower = refs[-3:]
    count, rows, _ = out_ref.shape
    half = len(orders[0]) // 2
    for side, order in enumerate(orders):
        @pl.when(pl.program_id(0) // 2 == side)
        def _():
            for k, (index, which) in enumerate(order):
                here = pl.ds(k * rows, rows)
                part = refs[side * half + index][:, which].reshape(count * rows, rows)
                left_upper[:, here], left_lower[:, here] = split(part)

    left = left_upper[...], left_lower[...]
    out_ref[...] = product(left, (upper[...], lower[...])).reshape(out_ref.shape)


def shared_rotated(previous, parts, orders, starts, right, shape):
    _, rows, orbitals = shape
    fresh = previous is None
    first, second = (start // 2 for start in starts)
    specs = []
    for side in range(2):
        turn_of = turns(side)
        specs += [
            pl.BlockSpec((2, 2, rows, rows), lambda i, t=turn_of: (t(i), 0, 0, 0))
        ] * len(parts[side])
    count = 2 + len(specs)
    return pl.pallas_call(
        functools.partial(shared_rotated_kernel, orders),
        grid=(4,),
        in_specs=[resident((orbitals, orbitals))] * 2
        + specs
        + ([] if fresh else [pl.BlockSpec(memory_space=pl.ANY)]),
        out_specs=pl.BlockSpec(
            (2, rows, orbitals), lambda i: (jnp.where(i < 2, first + i, second + i - 2), 0, 0)
        ),
        out_shape=jax.ShapeDtypeStruct(shape, f32),
        input_output_aliases={} if fresh else {count: 0},
        scratch_shapes=[pltpu.VMEM((2 * rows, orbitals), bf16)] * 2,
        cost_estimate=cost(12 * quad * rows * orbitals**2, 16 * quad * rows * orbitals),
        compiler_params=room,
        name="shared_rotated",
    )(*right, *parts[0], *parts[1], *([] if fresh else [previous]))


def second_terms_kernel(upper_ref, lower_ref, diagonal_ref, out_ref):
    total = jnp.zeros(out_ref.shape, f32)
    for p in range(upper_ref.shape[0]):
        left = upper_ref[p].astype(f32) + lower_ref[p].astype(f32)
        total = total + left * diagonal_ref[p]
    out_ref[...] = total


def second_terms(lefts, diagonal):
    vectors, rows, orbitals = lefts[0].shape
    size = 16
    block = pl.BlockSpec((vectors, size, orbitals), lambda i: (0, i, 0))
    return pl.pallas_call(
        second_terms_kernel,
        grid=(rows // size,),
        in_specs=[block, block, pl.BlockSpec((vectors, 1, orbitals), lambda i: (0, 0, 0))],
        out_specs=pl.BlockSpec((size, orbitals), lambda i: (i, 0)),
        out_shape=jax.ShapeDtypeStruct((rows, orbitals), f32),
        cost_estimate=cost(2 * lefts[0].size, 4 * lefts[0].size),
        compiler_params=room,
        name="second_terms",
    )(*lefts, diagonal)


def flip(x, k):
    count = lax.axis_size("vec")
    return lax.ppermute(x, "vec", [(i, i ^ k) for i in range(count)])


def sum_halves(part):
    bits = lax.axis_size("vec").bit_length() - 1
    masks = [2 ** (b + 1) - 1 for b in range(bits)]
    half = part.shape[0] // 2
    one, two = part[:half], part[half:]
    for turn_number, (a, b) in enumerate(zip(masks, reversed(masks))):
        one_more, two_more = flip(one, a), flip(two, b)
        one, two = one + one_more, two + two_more
        if turn_number == 0:
            first = one
    return jnp.concatenate([one, two], axis=0), first


def shards_of(part):
    out = []
    for k in range(0, lax.axis_size("row"), 2):
        mine = part if k == 0 else swap(part, k)
        out += [mine, swap(mine, 1)]
    return out


def after(x, *others):
    return lax.optimization_barrier((x,) + others)[0]


def tiled_shards(chol_vectors):
    shape = chol_vectors.shape
    vectors, _, _ = shape
    devices = lax.axis_size("row")
    me = lax.axis_index("row").astype(jnp.int32)[None]
    groups = shared_groups(vectors)
    plain = vectors - 2 * quad * groups
    bits = (devices // 2, devices // 4)
    everyone = list(range(devices))
    near = [[k for k in everyone if not k & bit] for bit in bits]
    orders = [
        [(near[s].index(k & ~bit), int(bool(k & bit))) for k in everyone]
        for s, bit in enumerate(bits)
    ]
    starts = [
        [plain + (s * groups + g) * quad for s in range(2)] for g in range(groups)
    ]

    early = {}

    def send_early(h, *others):
        g, i = h // 2, h % 2
        for s, bit in enumerate(bits):
            start = starts[g][s] + 2 * i
            early[g, s, i] = swap(after(own[start], *others), bit)

    def copy_own(source, halves):
        for h in halves:
            for s in range(2):
                start = starts[h // 2][s] + 2 * (h % 2)
                own[start] = source[start : start + 2]

    own = {}
    copy_own(chol_vectors, [0])
    part = gradient_terms(chol_vectors, me)
    part, first = sum_halves(part)
    send_early(0)
    copy_own(after(chol_vectors, first), range(1, 2 * groups))
    gathered = shards_of(part)
    send_early(1, *gathered)
    send_early(2, *gathered)
    *step, turned_upper, turned_lower = make_step(first_kernel, me, gathered, (), 4)
    lefts, diagonal = first_product(chol_vectors, step, me)
    diagonal = sum_over_row(diagonal)
    send_early(3, diagonal)
    part = second_terms(lefts, diagonal)
    part, _ = sum_halves(part)
    gathered = shards_of(part)
    for h in range(4, 2 * groups):
        send_early(h, *gathered)
    next_step = make_step(second_kernel, me, gathered, (turned_upper, turned_lower), 2)
    sent = plain_pieces(lefts, next_step, plain, devices)
    plain_parts = [sent[0]] + [swap(sent[k], k) for k in everyone[1:]]
    next_step = lax.optimization_barrier((*next_step, *sent))[:2]
    by_column, by_row, rotation = compose(me, step, next_step, devices)

    shared_parts = []

    for g in range(groups):
        others = [early[g, s, i] for s in range(2) for i in range(2)]
        sent = shared_pieces(near, chol_vectors, starts[g], others, by_column)
        shared_parts.append(
            [
                [pieces[0]]
                + [swap(pieces[i], near[s][i]) for i in range(1, len(near[s]))]
                for s, pieces in enumerate(sent)
            ]
        )
        by_column = lax.optimization_barrier((*by_column, *sent[0], *sent[1]))[:2]
    rotated = plain_rotated(shape, plain_parts, by_row)
    for g in range(groups):
        rotated = shared_rotated(rotated, shared_parts[g], orders, starts[g], by_row, shape)
    return rotated, rotation


def shared_groups(vectors):
    return (3 * vectors // 4) // (2 * quad)


def shards(chol_vectors):
    vectors, rows, _ = chol_vectors.shape
    devices, groups = lax.axis_size("row"), lax.axis_size("vec")
    tiled = rows % lane == 0 and vectors % (2 * quad) == 0 and devices >= 8
    if tiled and devices & (devices - 1) == 0 and groups & (groups - 1) == 0:
        return tiled_shards(chol_vectors)
    return plain_shards(chol_vectors)


def solution(mesh):
    return jax.shard_map(
        shards,
        mesh=mesh,
        in_specs=(P("vec", "row", None),),
        out_specs=(P("vec", "row", None), P("row", None)),
        check_vma=False,
    )
```

```python
import functools

import jax
import jax.numpy as jnp
from jax import lax
from jax.experimental import pallas as pl
from jax.experimental.pallas import tpu as pltpu
from jax.sharding import PartitionSpec as P


step_gain = 0.2
chunk_count = 4
high = lax.Precision.HIGH


def swap(x, k):
    count = lax.axis_size("row")
    return lax.ppermute(x, "row", [(i, i ^ k) for i in range(count)])


def turn(x, k):
    count = lax.axis_size("vec")
    return lax.ppermute(x, "vec", [(i, (i + k) % count) for i in range(count)])


def cut(x, index, size, axis):
    return lax.dynamic_slice_in_dim(x, index * size, size, axis)


def place(whole, part, index):
    return lax.dynamic_update_slice_in_dim(whole, part, index * part.shape[0], 0)


def sum_over_vec(part):
    count = lax.axis_size("vec")
    me = lax.axis_index("vec")
    size = part.shape[0] // count
    total = cut(part, me, size, 0)
    for k in range(1, count):
        total = total + turn(cut(part, (me + k) % count, size, 0), k)
    whole = place(jnp.zeros_like(part), total, me)
    for k in range(1, count):
        whole = place(whole, turn(total, k), (me - k) % count)
    return whole


def gather_rows(part):
    count = lax.axis_size("row")
    me = lax.axis_index("row")
    whole = jnp.zeros((count * part.shape[0], part.shape[1]), part.dtype)
    for k in range(0, count, 2):
        mine = part if k == 0 else swap(part, k)
        whole = place(whole, mine, me ^ k)
        whole = place(whole, swap(mine, 1), me ^ k ^ 1)
    return whole


def sum_over_row(part):
    pair = part + swap(part, 1)
    total = pair
    for k in range(2, lax.axis_size("row"), 2):
        total = total + swap(pair, k)
    return total


def step_of(gradient):
    orbitals = gradient.shape[0]
    norm = jnp.sqrt(jnp.sum(gradient * gradient) / (orbitals * orbitals) + 1e-06)
    generator = step_gain / jnp.sqrt(jnp.float32(orbitals)) * gradient / norm
    square = jnp.dot(generator, generator, precision=high)
    return jnp.eye(orbitals, dtype=jnp.float32) + generator + 0.5 * square


def plain_shards(chol_vectors):
    vectors, rows, orbitals = chol_vectors.shape
    devices = lax.axis_size("row")
    me = lax.axis_index("row")
    chunk = vectors // chunk_count

    block = cut(chol_vectors, me, rows, 2)
    here = jnp.eye(rows, dtype=jnp.bool_)
    diagonal = jnp.sum(jnp.where(here, block, 0.0), axis=2)
    part = jnp.sum(chol_vectors * diagonal[:, :, None], axis=0)
    terms = gather_rows(sum_over_vec(part))
    step = step_of(terms - terms.T)

    step_rows = cut(step, me, rows, 0)
    lefts = []
    part = jnp.zeros((rows, orbitals), jnp.float32)
    for c in range(chunk_count):
        own = chol_vectors[c * chunk : (c + 1) * chunk]
        left = jnp.einsum("pab,bm->pam", own, step, precision=high)
        lefts.append(left)
        diagonal = sum_over_row(jnp.sum(left * step_rows, axis=1))
        part = part + jnp.sum(left * diagonal[:, None, :], axis=0)
    terms = gather_rows(sum_over_vec(part))
    terms = lax.dot_general(step, terms, (((0,), (0,)), ((), ())), precision=high)
    step_next = step_of(terms.T - terms)
    rotation = jnp.dot(step, step_next, precision=high)
    order = me ^ jnp.arange(devices)
    rotation_order = rotation.reshape(devices, rows, orbitals)[order].reshape(orbitals, orbitals)

    outs = []
    for c in range(chunk_count):
        left = jnp.einsum("pab,bm->pam", lefts[c], step_next, precision=high)
        pieces = []
        for k in range(devices):
            piece = cut(left, me ^ k, rows, 2)
            pieces.append(piece if k == 0 else swap(piece, k))
        columns = jnp.concatenate(pieces, axis=1)
        outs.append(jnp.einsum("pam,ak->pmk", columns, rotation_order, precision=high))
    return jnp.concatenate(outs, axis=0), cut(rotation, me, rows, 0)


lane = 128
band = 256
quad = 4
bf16, f32 = jnp.bfloat16, jnp.float32


def split(x):
    upper = x.astype(bf16)
    return upper, (x - upper.astype(f32)).astype(bf16)


def product(left, right):
    dot = functools.partial(jnp.dot, preferred_element_type=f32)
    return dot(left[0], right[0]) + (dot(left[0], right[1]) + dot(left[1], right[0]))


def whole_spec():
    return pl.BlockSpec(memory_space=pltpu.VMEM)


def resident(shape):
    return pl.BlockSpec(shape, lambda i: (0,) * len(shape), pipeline_mode=pl.Buffered(1))


def room(mebibytes):
    return pltpu.CompilerParams(vmem_limit_bytes=mebibytes << 20)


def cost(flops, data):
    return pl.CostEstimate(flops=flops, bytes_accessed=data, transcendentals=0)


def gradient_kernel(me_ref, vectors_ref, slab_ref, out_ref):
    size, width = slab_ref.shape[1:]
    row = lax.broadcasted_iota(jnp.int32, (size, width), 0) + pl.program_id(0) * size
    here = lax.broadcasted_iota(jnp.int32, (size, width), 1) == row
    total = jnp.zeros(out_ref.shape, f32)
    for p in range(vectors_ref.shape[0]):
        diagonal = jnp.sum(jnp.where(here, slab_ref[p], 0.0), axis=1, keepdims=True)
        total = total + vectors_ref[p] * diagonal
    out_ref[...] = total


def gradient_terms(chol_vectors, me):
    vectors, rows, orbitals = chol_vectors.shape
    size = 16
    return pl.pallas_call(
        gradient_kernel,
        grid_spec=pltpu.PrefetchScalarGridSpec(
            num_scalar_prefetch=1,
            grid=(rows // size,),
            in_specs=[
                pl.BlockSpec((vectors, size, orbitals), lambda i, me: (0, i, 0)),
                pl.BlockSpec((vectors, size, rows), lambda i, me: (0, i, me[0])),
            ],
            out_specs=pl.BlockSpec((size, orbitals), lambda i, me: (i, 0)),
        ),
        out_shape=jax.ShapeDtypeStruct((rows, orbitals), f32),
        cost_estimate=cost(2 * chol_vectors.size, 4 * chol_vectors.size),
        compiler_params=room(10),
        name="gradient_terms",
    )(me, chol_vectors, chol_vectors)


def skew_part(terms_ref, sign, skew_ref, upper_ref, lower_ref):
    def body(i, total):
        at = pl.ds(pl.multiple_of(i * lane, lane), lane)
        skew = sign * (terms_ref[at, :] - terms_ref[:, at].T)
        skew_ref[at, :] = skew
        upper_ref[at, :], lower_ref[at, :] = split(skew)
        return total + jnp.sum(skew * skew, axis=(0, 1), keepdims=True)

    return lax.fori_loop(0, skew_ref.shape[0] // lane, body, jnp.zeros((1, 1), f32))


def columns_of(t, width):
    return pl.ds(pl.multiple_of(t * width, width), width)


def step_parts(total, skew_ref, upper_ref, lower_ref, store):
    orbitals = skew_ref.shape[0]
    norm = jnp.sqrt(total / (orbitals * orbitals) + 1e-06)
    scale = step_gain / jnp.sqrt(jnp.full((1, 1), orbitals, f32)) / norm

    @pl.loop(0, orbitals // band)
    def _(t):
        at = columns_of(t, band)
        square = product(
            (upper_ref[...], lower_ref[...]), (upper_ref[:, at], lower_ref[:, at])
        )
        row = lax.broadcasted_iota(jnp.int32, (orbitals, band), 0)
        column = lax.broadcasted_iota(jnp.int32, (orbitals, band), 1) + t * band
        even = jnp.where(row == column, 1.0, 0.0) + (0.5 * scale * scale) * square
        store(t, at, even, scale * skew_ref[:, at])


def first_kernel(devices, me_ref, *refs):
    shards, refs = refs[:devices], refs[devices:]
    step, turned = refs[:2], refs[2:4]
    terms, skew, upper, lower = refs[4:]
    half = shards[0].shape[0]
    for i, shard in enumerate(shards):
        start = (me_ref[0] ^ (i // 2)) * (2 * half) + i % 2 * half
        terms[pl.ds(pl.multiple_of(start, half), half), :] = shard[...]
    total = skew_part(terms, 1.0, skew, upper, lower)

    def store(t, at, even, odd):
        step[0][:, at], step[1][:, at] = split(even + odd)
        turned[0][:, at], turned[1][:, at] = split(even - odd)

    step_parts(total, skew, upper, lower, store)


def second_kernel(devices, me_ref, *refs):
    shards, turned, refs = refs[:devices], refs[devices : devices + 2], refs[devices + 2 :]
    ordered, (terms, skew, upper, lower) = refs[:2], refs[2:]
    half = shards[0].shape[0]
    rows = 2 * half
    orbitals = terms.shape[0]
    me = me_ref[0]
    for i, shard in enumerate(shards):
        at = pl.ds(pl.multiple_of((me ^ (i // 2)) * rows + i % 2 * half, half), half)
        upper[at, :], lower[at, :] = split(shard[...])

    @pl.loop(0, orbitals // band)
    def _(t):
        at = columns_of(t, band)
        terms[:, at] = product(
            (turned[0][...], turned[1][...]), (upper[:, at], lower[:, at])
        )

    total = skew_part(terms, -1.0, skew, upper, lower)

    def store(t, at, even, odd):
        whole = even + odd
        for b in range(band // rows):
            column = t * (band // rows) + b
            here = pl.ds(pl.multiple_of((me ^ column) * rows, rows), rows)
            part = whole[:, b * rows : (b + 1) * rows]
            ordered[0][:, here], ordered[1][:, here] = split(part)

    step_parts(total, skew, upper, lower, store)


def make_step(kernel, me, shards, extra, count):
    devices = len(shards)
    orbitals = shards[0].shape[1]
    square = (orbitals, orbitals)
    part = jax.ShapeDtypeStruct(square, bf16)
    return pl.pallas_call(
        functools.partial(kernel, devices),
        in_specs=[pl.BlockSpec(memory_space=pltpu.SMEM)]
        + [whole_spec()] * (devices + len(extra)),
        out_specs=[whole_spec()] * count,
        out_shape=[part] * count,
        scratch_shapes=[
            pltpu.VMEM(square, f32),
            pltpu.VMEM(square, f32),
            pltpu.VMEM(square, bf16),
            pltpu.VMEM(square, bf16),
        ],
        cost_estimate=cost(12 * orbitals**3, 24 * orbitals**2),
        compiler_params=room(18),
    )(me, *shards, *extra)


def compose_kernel(devices, me_ref, left_upper, left_lower, right_upper, right_lower, *refs):
    by_column, by_row, own_ref, whole = refs[:2], refs[2:4], refs[4], refs[5]
    rows = own_ref.shape[0]
    orbitals = whole.shape[0]
    me = me_ref[0]

    @pl.loop(0, orbitals // band)
    def _(t):
        at = columns_of(t, band)
        value = product(
            (left_upper[...], left_lower[...]), (right_upper[:, at], right_lower[:, at])
        )
        by_column[0][:, at], by_column[1][:, at] = split(value)
        for b in range(band // rows):
            column = t * (band // rows) + b
            here = pl.ds(pl.multiple_of((me ^ column) * rows, rows), rows)
            whole[:, here] = value[:, b * rows : (b + 1) * rows]

    own_ref[...] = whole[pl.ds(pl.multiple_of(me * rows, rows), rows), :]
    for k in range(devices):
        source = pl.ds(pl.multiple_of((me ^ k) * rows, rows), rows)
        here = pl.ds(k * rows, rows)
        by_row[0][here, :], by_row[1][here, :] = split(whole[source, :])


def compose(me, left, right, devices):
    orbitals = left[0].shape[0]
    square = (orbitals, orbitals)
    part = jax.ShapeDtypeStruct(square, bf16)
    out = pl.pallas_call(
        functools.partial(compose_kernel, devices),
        in_specs=[pl.BlockSpec(memory_space=pltpu.SMEM)] + [whole_spec()] * 4,
        out_specs=[whole_spec()] * 5,
        out_shape=[part] * 4 + [jax.ShapeDtypeStruct((orbitals // devices, orbitals), f32)],
        scratch_shapes=[pltpu.VMEM(square, f32)],
        cost_estimate=cost(6 * orbitals**3, 16 * orbitals**2),
        compiler_params=room(14),
        name="compose",
    )(me, *left, *right)
    return out[:2], out[2:4], out[4]


def first_product_kernel(me_ref, vectors_ref, upper, lower, rows_upper, rows_lower, out_upper, out_lower, diagonal):
    size, rows, orbitals = vectors_ref.shape
    own = rows_upper[...].astype(f32) + rows_lower[...].astype(f32)
    vectors = vectors_ref[...].reshape(size * rows, orbitals)
    left = product(split(vectors), (upper[...], lower[...])).reshape(size, rows, orbitals)
    out_upper[...], out_lower[...] = split(left)
    diagonal[...] = jnp.sum(left * own[None], axis=1, keepdims=True)


def first_product(chol_vectors, step, me):
    vectors, rows, orbitals = chol_vectors.shape
    part = jax.ShapeDtypeStruct(chol_vectors.shape, bf16)
    block = pl.BlockSpec((quad, rows, orbitals), lambda i, me: (i, 0, 0))
    square = pl.BlockSpec(
        (orbitals, orbitals), lambda i, me: (0, 0), pipeline_mode=pl.Buffered(1)
    )
    own = pl.BlockSpec((rows, orbitals), lambda i, me: (me[0], 0))
    out = pl.pallas_call(
        first_product_kernel,
        grid_spec=pltpu.PrefetchScalarGridSpec(
            num_scalar_prefetch=1,
            grid=(vectors // quad,),
            in_specs=[block, square, square, own, own],
            out_specs=[block, block, pl.BlockSpec((quad, 1, orbitals), lambda i, me: (i, 0, 0))],
        ),
        out_shape=[part, part, jax.ShapeDtypeStruct((vectors, 1, orbitals), f32)],
        cost_estimate=cost(6 * chol_vectors.size * orbitals, 8 * chol_vectors.size),
        compiler_params=room(20),
        name="first_product",
    )(me, chol_vectors, *step, *step)
    return out[:2], out[2]


def pack_kernel(kept, me_ref, one, two, one_out, two_out):
    rows = one.shape[1]
    for source, out, blocks in ((one, one_out, kept[0]), (two, two_out, kept[1])):
        for j, k in enumerate(blocks):
            at = pl.ds(pl.multiple_of((me_ref[0] ^ k) * rows, rows), rows)
            out[:, :, j * rows : (j + 1) * rows] = source[:, :, at]


def pack(chol_vectors, me, kept, first, count):
    vectors, rows, orbitals = chol_vectors.shape
    width = len(kept[0]) * rows
    second = vectors // 2 + first
    out = pl.BlockSpec((2, rows, width), lambda i, me: (i, 0, 0))
    return pl.pallas_call(
        functools.partial(pack_kernel, kept),
        grid_spec=pltpu.PrefetchScalarGridSpec(
            num_scalar_prefetch=1,
            grid=(count // 2,),
            in_specs=[
                pl.BlockSpec((2, rows, orbitals), lambda i, me: (i + first // 2, 0, 0)),
                pl.BlockSpec((2, rows, orbitals), lambda i, me: (i + second // 2, 0, 0)),
            ],
            out_specs=[out, out],
        ),
        out_shape=[jax.ShapeDtypeStruct((count, rows, width), f32)] * 2,
        cost_estimate=cost(0, 16 * count * rows * orbitals),
        compiler_params=room(10),
        name="pack",
    )(me, chol_vectors, chol_vectors)


def siblings_kernel(me_ref, one, two, one_out, two_out):
    one_out[...] = one[...]
    two_out[...] = two[...]


def for_siblings(chol_vectors, me, bits):
    vectors, rows, _ = chol_vectors.shape
    steps = vectors // 2 // quad
    block = (quad, rows, rows)
    out = pl.BlockSpec(block, lambda i, me: (i, 0, 0))
    return pl.pallas_call(
        siblings_kernel,
        grid_spec=pltpu.PrefetchScalarGridSpec(
            num_scalar_prefetch=1,
            grid=(steps,),
            in_specs=[
                pl.BlockSpec(block, lambda i, me, s=s, b=b: (s * steps + i, 0, me[0] ^ b ^ 1))
                for s, b in enumerate(bits)
            ],
            out_specs=[out, out],
        ),
        out_shape=[jax.ShapeDtypeStruct((vectors // 2, rows, rows), f32)] * 2,
        cost_estimate=cost(0, 8 * vectors * rows * rows),
        compiler_params=room(6),
        name="for_siblings",
    )(me, chol_vectors, chol_vectors)


def turns(side):
    return (lambda i: jnp.minimum(i, 1)) if side == 0 else (lambda i: jnp.maximum(i - 2, 0))


def shared_pieces_kernel(bits, kept, me_ref, own, *refs):
    others, siblings, (upper, lower), refs = refs[:4], refs[4:6], refs[6:8], refs[8:]
    outs, (left_upper, left_lower, blocks) = refs[:-3], refs[-3:]
    count, rows, orbitals = own.shape
    pair = orbitals // 4
    half = len(outs) // 2
    step = pl.program_id(0)
    size = count * rows
    me = me_ref[0]

    def put(block, start, column):
        at = pl.ds(pl.multiple_of(column * rows, rows), rows)
        here = pl.ds(start, block.shape[0])
        left_upper[here, at], left_lower[here, at] = split(block)

    left_upper[:size], left_lower[:size] = split(own[...].reshape(size, orbitals))
    for i, other in enumerate(others):
        @pl.when(step == i)
        def _():
            for j, k in enumerate(kept[i // 2]):
                block = other[:, :, j * rows : (j + 1) * rows].reshape(size, rows)
                put(block, size, me ^ bits[i // 2] ^ k)

    for side in range(2):
        @pl.when(step // 2 == side)
        def _():
            at = pl.ds(pl.multiple_of((me ^ bits[side]) * rows, rows), rows)
            for p in range(count):
                put(own[p, :, at].T, size + p * rows, me)
                put(siblings[side][p].T, size + p * rows, me ^ 1)

    left = left_upper[...], left_lower[...]
    middle = pl.ds(pl.multiple_of((1 + step // 2) * pair, pair), pair)
    for n, at in enumerate((pl.ds(0, pair), middle)):
        value = product(left, (upper[:, at], lower[:, at]))
        for b in range(half // 2):
            for p in range(2 * count):
                block = value[p * rows : (p + 1) * rows, b * rows : (b + 1) * rows]
                blocks[n * (half // 2) + b, p % count, p // count] = block.T
    for side in range(2):
        @pl.when(step // 2 == side)
        def _():
            for b in range(half):
                outs[side * half + b][...] = blocks[b]


def shared_pieces(bits, kept, near, me, chol_vectors, starts, others, siblings, right):
    _, rows, orbitals = chol_vectors.shape
    half = len(near[0])
    first, second = (start // 2 for start in starts)
    specs = [
        pl.BlockSpec(
            (2, rows, orbitals),
            lambda i, me: (jnp.where(i < 2, first + i, second + i - 2), 0, 0),
        )
    ]
    for x, which in others:
        specs.append(
            pl.BlockSpec(
                (2,) + x.shape[1:], lambda i, me, w=which: (w, 0, 0), pipeline_mode=pl.Buffered(1)
            )
        )
    outs = []
    for side in range(2):
        turn_of = turns(side)
        specs.append(
            pl.BlockSpec((2, rows, rows), lambda i, me, t=turn_of: (first + t(i), 0, 0))
        )
        outs += [
            pl.BlockSpec((2, 2, rows, rows), lambda i, me, t=turn_of: (t(i), 0, 0, 0))
        ] * half
    square = pl.BlockSpec(
        (orbitals, orbitals), lambda i, me: (0, 0), pipeline_mode=pl.Buffered(1)
    )
    out = pl.pallas_call(
        functools.partial(shared_pieces_kernel, bits, kept),
        grid_spec=pltpu.PrefetchScalarGridSpec(
            num_scalar_prefetch=1,
            grid=(4,),
            in_specs=specs + [square] * 2,
            out_specs=outs,
            scratch_shapes=[
                pltpu.VMEM((4 * rows, orbitals), bf16),
                pltpu.VMEM((4 * rows, orbitals), bf16),
                pltpu.VMEM((half, 2, 2, rows, rows), f32),
            ],
        ),
        out_shape=[jax.ShapeDtypeStruct((quad, 2, rows, rows), f32)] * (2 * half),
        cost_estimate=cost(
            12 * quad * rows * orbitals**2, 16 * quad * rows * orbitals
        ),
        compiler_params=room(32),
        name="shared_pieces",
    )(me, chol_vectors, *(x for x, _ in others), *siblings, *right)
    return out[:half], out[half:]


def shared_rotated_kernel(orders, upper, lower, *refs):
    out_ref, left_upper, left_lower = refs[-3:]
    count, rows, _ = out_ref.shape
    half = len(orders[0]) // 2
    for side, order in enumerate(orders):
        @pl.when(pl.program_id(0) // 2 == side)
        def _():
            for k, (index, which) in enumerate(order):
                here = pl.ds(k * rows, rows)
                part = refs[side * half + index][:, which].reshape(count * rows, rows)
                left_upper[:, here], left_lower[:, here] = split(part)

    left = left_upper[...], left_lower[...]
    out_ref[...] = product(left, (upper[...], lower[...])).reshape(out_ref.shape)


def shared_rotated(previous, parts, orders, starts, right, shape):
    _, rows, orbitals = shape
    fresh = previous is None
    first, second = (start // 2 for start in starts)
    specs = []
    for side in range(2):
        turn_of = turns(side)
        specs += [
            pl.BlockSpec((2, 2, rows, rows), lambda i, t=turn_of: (t(i), 0, 0, 0))
        ] * len(parts[side])
    count = 2 + len(specs)
    return pl.pallas_call(
        functools.partial(shared_rotated_kernel, orders),
        grid=(4,),
        in_specs=[resident((orbitals, orbitals))] * 2
        + specs
        + ([] if fresh else [pl.BlockSpec(memory_space=pl.ANY)]),
        out_specs=pl.BlockSpec(
            (2, rows, orbitals), lambda i: (jnp.where(i < 2, first + i, second + i - 2), 0, 0)
        ),
        out_shape=jax.ShapeDtypeStruct(shape, f32),
        input_output_aliases={} if fresh else {count: 0},
        scratch_shapes=[pltpu.VMEM((2 * rows, orbitals), bf16)] * 2,
        cost_estimate=cost(12 * quad * rows * orbitals**2, 16 * quad * rows * orbitals),
        compiler_params=room(16),
        name="shared_rotated",
    )(*right, *parts[0], *parts[1], *([] if fresh else [previous]))


def second_terms_kernel(upper_ref, lower_ref, diagonal_ref, out_ref):
    total = jnp.zeros(out_ref.shape, f32)
    for p in range(upper_ref.shape[0]):
        left = upper_ref[p].astype(f32) + lower_ref[p].astype(f32)
        total = total + left * diagonal_ref[p]
    out_ref[...] = total


def second_terms(lefts, diagonal):
    vectors, rows, orbitals = lefts[0].shape
    size = 16
    block = pl.BlockSpec((vectors, size, orbitals), lambda i: (0, i, 0))
    return pl.pallas_call(
        second_terms_kernel,
        grid=(rows // size,),
        in_specs=[block, block, pl.BlockSpec((vectors, 1, orbitals), lambda i: (0, 0, 0))],
        out_specs=pl.BlockSpec((size, orbitals), lambda i: (i, 0)),
        out_shape=jax.ShapeDtypeStruct((rows, orbitals), f32),
        cost_estimate=cost(2 * lefts[0].size, 4 * lefts[0].size),
        compiler_params=room(8),
        name="second_terms",
    )(*lefts, diagonal)


def flip(x, k):
    count = lax.axis_size("vec")
    return lax.ppermute(x, "vec", [(i, i ^ k) for i in range(count)])


def sum_halves(part):
    bits = lax.axis_size("vec").bit_length() - 1
    masks = [2 ** (b + 1) - 1 for b in range(bits)]
    half = part.shape[0] // 2
    one, two = part[:half], part[half:]
    for a, b in zip(masks, reversed(masks)):
        one_more, two_more = flip(one, a), flip(two, b)
        one, two = one + one_more, two + two_more
    return one, two


def shards_of(one, two):
    high, low = lax.axis_size("row") // 2, lax.axis_size("row") // 4
    one_low, two_high = swap(one, low), swap(two, high)
    one_high, two_low = swap(one, high), swap(two, low)
    one_both, two_both = swap(one_low, high), swap(two_high, low)
    halves = {
        0: (one, two),
        low: (one_low, two_low),
        high: (one_high, two_high),
        low | high: (one_both, two_both),
    }
    out = []
    for k in sorted(halves):
        out += [*halves[k], *(swap(x, 1) for x in halves[k])]
    return out


def after(x, *others):
    return lax.optimization_barrier((x,) + others)[0]


def tiled_shards(chol_vectors):
    shape = chol_vectors.shape
    vectors, _, _ = shape
    devices = lax.axis_size("row")
    me = lax.axis_index("row").astype(jnp.int32)[None]
    middle = vectors // 2
    bits = (devices // 2, devices // 4)
    everyone = list(range(devices))
    near = [[k for k in everyone if not k & bit] for bit in bits]
    kept = [[k for k in everyone if k not in (bit, bit ^ 1)] for bit in bits]
    orders = [
        [(near[s].index(k & ~bit), int(bool(k & bit))) for k in everyone]
        for s, bit in enumerate(bits)
    ]

    eighth = middle // 8
    packed, place_of = [], []
    for part, count in enumerate((eighth, 3 * eighth, 2 * eighth, 2 * eighth)):
        start = len(place_of) * 2
        packed.append(pack(chol_vectors, me, kept, start, count))
        place_of += [(part, i) for i in range(count // 2)]
    blocks = for_siblings(chol_vectors, me, bits)
    early = []

    def send_early(*others):
        part = len(early)
        early.append(
            [swap(after(x, *others), bit) for x, bit in zip(packed[part], bits)]
        )

    part = gradient_terms(chol_vectors, me)
    halves = sum_halves(part)
    send_early()
    siblings = [swap(x, 1) for x in blocks]
    gathered = shards_of(*halves)
    send_early(*gathered)
    *step, turned_upper, turned_lower = make_step(first_kernel, me, gathered, (), 4)
    lefts, diagonal = first_product(chol_vectors, step, me)
    diagonal = sum_over_row(diagonal)
    send_early(diagonal)
    part = second_terms(lefts, diagonal)
    gathered = shards_of(*sum_halves(part))
    send_early(*gathered)
    next_step = make_step(second_kernel, me, gathered, (turned_upper, turned_lower), 2)
    by_column, by_row, rotation = compose(me, step, next_step, devices)

    groups = middle // quad
    starts = [(g * quad, middle + g * quad) for g in range(groups)]
    parts = []

    for g in range(groups):
        others = []
        for s in range(2):
            for h in (2 * g, 2 * g + 1):
                window, which = place_of[h]
                others.append((early[window][s], which))
        sent = shared_pieces(
            bits, kept, near, me, chol_vectors, starts[g], others, siblings, by_column
        )
        parts.append(
            [
                [pieces[0]]
                + [swap(pieces[i], near[s][i]) for i in range(1, len(near[s]))]
                for s, pieces in enumerate(sent)
            ]
        )
        by_column = lax.optimization_barrier((*by_column, *sent[0], *sent[1]))[:2]
    rotated = None
    for g in range(groups):
        rotated = shared_rotated(rotated, parts[g], orders, starts[g], by_row, shape)
    return rotated, rotation


def shards(chol_vectors):
    vectors, rows, _ = chol_vectors.shape
    devices, groups = lax.axis_size("row"), lax.axis_size("vec")
    tiled = rows % lane == 0 and vectors % (8 * quad) == 0 and devices == 8
    if tiled and groups & (groups - 1) == 0:
        return tiled_shards(chol_vectors)
    return plain_shards(chol_vectors)


def solution(mesh):
    return jax.shard_map(
        shards,
        mesh=mesh,
        in_specs=(P("vec", "row", None),),
        out_specs=(P("vec", "row", None), P("row", None)),
        check_vma=False,
    )
```

```python
import functools

import jax
import jax.numpy as jnp
from jax import lax
from jax.experimental import pallas as pl
from jax.experimental.pallas import tpu as pltpu
from jax.sharding import PartitionSpec as P


step_gain = 0.2
chunk_count = 4
high = lax.Precision.HIGH


def swap(x, k):
    count = lax.axis_size("row")
    return lax.ppermute(x, "row", [(i, i ^ k) for i in range(count)])


def turn(x, k):
    count = lax.axis_size("vec")
    return lax.ppermute(x, "vec", [(i, (i + k) % count) for i in range(count)])


def cut(x, index, size, axis):
    return lax.dynamic_slice_in_dim(x, index * size, size, axis)


def place(whole, part, index):
    return lax.dynamic_update_slice_in_dim(whole, part, index * part.shape[0], 0)


def sum_over_vec(part):
    count = lax.axis_size("vec")
    me = lax.axis_index("vec")
    size = part.shape[0] // count
    total = cut(part, me, size, 0)
    for k in range(1, count):
        total = total + turn(cut(part, (me + k) % count, size, 0), k)
    whole = place(jnp.zeros_like(part), total, me)
    for k in range(1, count):
        whole = place(whole, turn(total, k), (me - k) % count)
    return whole


def gather_rows(part):
    count = lax.axis_size("row")
    me = lax.axis_index("row")
    whole = jnp.zeros((count * part.shape[0], part.shape[1]), part.dtype)
    for k in range(0, count, 2):
        mine = part if k == 0 else swap(part, k)
        whole = place(whole, mine, me ^ k)
        whole = place(whole, swap(mine, 1), me ^ k ^ 1)
    return whole


def sum_over_row(part):
    pair = part + swap(part, 1)
    total = pair
    for k in range(2, lax.axis_size("row"), 2):
        total = total + swap(pair, k)
    return total


def step_of(gradient):
    orbitals = gradient.shape[0]
    norm = jnp.sqrt(jnp.sum(gradient * gradient) / (orbitals * orbitals) + 1e-06)
    generator = step_gain / jnp.sqrt(jnp.float32(orbitals)) * gradient / norm
    square = jnp.dot(generator, generator, precision=high)
    return jnp.eye(orbitals, dtype=jnp.float32) + generator + 0.5 * square


def plain_shards(chol_vectors):
    vectors, rows, orbitals = chol_vectors.shape
    devices = lax.axis_size("row")
    me = lax.axis_index("row")
    chunk = vectors // chunk_count

    block = cut(chol_vectors, me, rows, 2)
    here = jnp.eye(rows, dtype=jnp.bool_)
    diagonal = jnp.sum(jnp.where(here, block, 0.0), axis=2)
    part = jnp.sum(chol_vectors * diagonal[:, :, None], axis=0)
    terms = gather_rows(sum_over_vec(part))
    step = step_of(terms - terms.T)

    step_rows = cut(step, me, rows, 0)
    lefts = []
    part = jnp.zeros((rows, orbitals), jnp.float32)
    for c in range(chunk_count):
        own = chol_vectors[c * chunk : (c + 1) * chunk]
        left = jnp.einsum("pab,bm->pam", own, step, precision=high)
        lefts.append(left)
        diagonal = sum_over_row(jnp.sum(left * step_rows, axis=1))
        part = part + jnp.sum(left * diagonal[:, None, :], axis=0)
    terms = gather_rows(sum_over_vec(part))
    terms = lax.dot_general(step, terms, (((0,), (0,)), ((), ())), precision=high)
    step_next = step_of(terms.T - terms)
    rotation = jnp.dot(step, step_next, precision=high)
    order = me ^ jnp.arange(devices)
    rotation_order = rotation.reshape(devices, rows, orbitals)[order].reshape(orbitals, orbitals)

    outs = []
    for c in range(chunk_count):
        left = jnp.einsum("pab,bm->pam", lefts[c], step_next, precision=high)
        pieces = []
        for k in range(devices):
            piece = cut(left, me ^ k, rows, 2)
            pieces.append(piece if k == 0 else swap(piece, k))
        columns = jnp.concatenate(pieces, axis=1)
        outs.append(jnp.einsum("pam,ak->pmk", columns, rotation_order, precision=high))
    return jnp.concatenate(outs, axis=0), cut(rotation, me, rows, 0)


lane = 128
band = 256
quad = 4
bf16, f32 = jnp.bfloat16, jnp.float32


def split(x):
    upper = x.astype(bf16)
    return upper, (x - upper.astype(f32)).astype(bf16)


def product(left, right):
    dot = functools.partial(jnp.dot, preferred_element_type=f32)
    return dot(left[0], right[0]) + (dot(left[0], right[1]) + dot(left[1], right[0]))


def whole_spec():
    return pl.BlockSpec(memory_space=pltpu.VMEM)


def resident(shape):
    return pl.BlockSpec(shape, lambda i: (0,) * len(shape), pipeline_mode=pl.Buffered(1))


def room(mebibytes):
    return pltpu.CompilerParams(vmem_limit_bytes=mebibytes << 20)


def cost(flops, data):
    return pl.CostEstimate(flops=flops, bytes_accessed=data, transcendentals=0)


def gradient_kernel(me_ref, vectors_ref, slab_ref, out_ref):
    size, width = slab_ref.shape[1:]
    row = lax.broadcasted_iota(jnp.int32, (size, width), 0) + pl.program_id(0) * size
    here = lax.broadcasted_iota(jnp.int32, (size, width), 1) == row
    total = jnp.zeros(out_ref.shape, f32)
    for p in range(vectors_ref.shape[0]):
        diagonal = jnp.sum(jnp.where(here, slab_ref[p], 0.0), axis=1, keepdims=True)
        total = total + vectors_ref[p] * diagonal
    out_ref[...] = total


def gradient_terms(chol_vectors, me):
    vectors, rows, orbitals = chol_vectors.shape
    size = 16
    return pl.pallas_call(
        gradient_kernel,
        grid_spec=pltpu.PrefetchScalarGridSpec(
            num_scalar_prefetch=1,
            grid=(rows // size,),
            in_specs=[
                pl.BlockSpec((vectors, size, orbitals), lambda i, me: (0, i, 0)),
                pl.BlockSpec((vectors, size, rows), lambda i, me: (0, i, me[0])),
            ],
            out_specs=pl.BlockSpec((size, orbitals), lambda i, me: (i, 0)),
        ),
        out_shape=jax.ShapeDtypeStruct((rows, orbitals), f32),
        cost_estimate=cost(2 * chol_vectors.size, 4 * chol_vectors.size),
        compiler_params=room(10),
        name="gradient_terms",
    )(me, chol_vectors, chol_vectors)


def skew_part(terms_ref, sign, skew_ref, upper_ref, lower_ref):
    def body(i, total):
        at = pl.ds(pl.multiple_of(i * lane, lane), lane)
        skew = sign * (terms_ref[at, :] - terms_ref[:, at].T)
        skew_ref[at, :] = skew
        upper_ref[at, :], lower_ref[at, :] = split(skew)
        return total + jnp.sum(skew * skew, axis=(0, 1), keepdims=True)

    return lax.fori_loop(0, skew_ref.shape[0] // lane, body, jnp.zeros((1, 1), f32))


def columns_of(t, width):
    return pl.ds(pl.multiple_of(t * width, width), width)


def step_parts(total, skew_ref, upper_ref, lower_ref, store):
    orbitals = skew_ref.shape[0]
    norm = jnp.sqrt(total / (orbitals * orbitals) + 1e-06)
    scale = step_gain / jnp.sqrt(jnp.full((1, 1), orbitals, f32)) / norm

    @pl.loop(0, orbitals // band)
    def _(t):
        at = columns_of(t, band)
        square = product(
            (upper_ref[...], lower_ref[...]), (upper_ref[:, at], lower_ref[:, at])
        )
        row = lax.broadcasted_iota(jnp.int32, (orbitals, band), 0)
        column = lax.broadcasted_iota(jnp.int32, (orbitals, band), 1) + t * band
        even = jnp.where(row == column, 1.0, 0.0) + (0.5 * scale * scale) * square
        store(t, at, even, scale * skew_ref[:, at])


def first_kernel(devices, me_ref, *refs):
    shards, refs = refs[:devices], refs[devices:]
    step, turned = refs[:2], refs[2:4]
    terms, skew, upper, lower = refs[4:]
    half = shards[0].shape[0]
    for i, shard in enumerate(shards):
        start = (me_ref[0] ^ (i // 2)) * (2 * half) + i % 2 * half
        terms[pl.ds(pl.multiple_of(start, half), half), :] = shard[...]
    total = skew_part(terms, 1.0, skew, upper, lower)

    def store(t, at, even, odd):
        step[0][:, at], step[1][:, at] = split(even + odd)
        turned[0][:, at], turned[1][:, at] = split(even - odd)

    step_parts(total, skew, upper, lower, store)


def second_kernel(devices, me_ref, *refs):
    shards, turned, refs = refs[:devices], refs[devices : devices + 2], refs[devices + 2 :]
    ordered, (terms, skew, upper, lower) = refs[:2], refs[2:]
    half = shards[0].shape[0]
    rows = 2 * half
    orbitals = terms.shape[0]
    me = me_ref[0]
    for i, shard in enumerate(shards):
        at = pl.ds(pl.multiple_of((me ^ (i // 2)) * rows + i % 2 * half, half), half)
        upper[at, :], lower[at, :] = split(shard[...])

    @pl.loop(0, orbitals // band)
    def _(t):
        at = columns_of(t, band)
        terms[:, at] = product(
            (turned[0][...], turned[1][...]), (upper[:, at], lower[:, at])
        )

    total = skew_part(terms, -1.0, skew, upper, lower)

    def store(t, at, even, odd):
        whole = even + odd
        for b in range(band // rows):
            column = t * (band // rows) + b
            here = pl.ds(pl.multiple_of((me ^ column) * rows, rows), rows)
            part = whole[:, b * rows : (b + 1) * rows]
            ordered[0][:, here], ordered[1][:, here] = split(part)

    step_parts(total, skew, upper, lower, store)


def make_step(kernel, me, shards, extra, count):
    devices = len(shards)
    orbitals = shards[0].shape[1]
    square = (orbitals, orbitals)
    part = jax.ShapeDtypeStruct(square, bf16)
    return pl.pallas_call(
        functools.partial(kernel, devices),
        in_specs=[pl.BlockSpec(memory_space=pltpu.SMEM)]
        + [whole_spec()] * (devices + len(extra)),
        out_specs=[whole_spec()] * count,
        out_shape=[part] * count,
        scratch_shapes=[
            pltpu.VMEM(square, f32),
            pltpu.VMEM(square, f32),
            pltpu.VMEM(square, bf16),
            pltpu.VMEM(square, bf16),
        ],
        cost_estimate=cost(12 * orbitals**3, 24 * orbitals**2),
        compiler_params=room(18),
    )(me, *shards, *extra)


def compose_kernel(devices, me_ref, left_upper, left_lower, right_upper, right_lower, *refs):
    by_column, by_row, own_ref, whole = refs[:2], refs[2:4], refs[4], refs[5]
    rows = own_ref.shape[0]
    orbitals = whole.shape[0]
    me = me_ref[0]

    @pl.loop(0, orbitals // band)
    def _(t):
        at = columns_of(t, band)
        value = product(
            (left_upper[...], left_lower[...]), (right_upper[:, at], right_lower[:, at])
        )
        by_column[0][:, at], by_column[1][:, at] = split(value)
        for b in range(band // rows):
            column = t * (band // rows) + b
            here = pl.ds(pl.multiple_of((me ^ column) * rows, rows), rows)
            whole[:, here] = value[:, b * rows : (b + 1) * rows]

    own_ref[...] = whole[pl.ds(pl.multiple_of(me * rows, rows), rows), :]
    for k in range(devices):
        source = pl.ds(pl.multiple_of((me ^ k) * rows, rows), rows)
        here = pl.ds(k * rows, rows)
        by_row[0][here, :], by_row[1][here, :] = split(whole[source, :])


def compose(me, left, right, devices):
    orbitals = left[0].shape[0]
    square = (orbitals, orbitals)
    part = jax.ShapeDtypeStruct(square, bf16)
    out = pl.pallas_call(
        functools.partial(compose_kernel, devices),
        in_specs=[pl.BlockSpec(memory_space=pltpu.SMEM)] + [whole_spec()] * 4,
        out_specs=[whole_spec()] * 5,
        out_shape=[part] * 4 + [jax.ShapeDtypeStruct((orbitals // devices, orbitals), f32)],
        scratch_shapes=[pltpu.VMEM(square, f32)],
        cost_estimate=cost(6 * orbitals**3, 16 * orbitals**2),
        compiler_params=room(16),
        name="compose",
    )(me, *left, *right)
    return out[:2], out[2:4], out[4]


def first_product_kernel(me_ref, vectors_ref, upper, lower, rows_upper, rows_lower, out_upper, out_lower, diagonal):
    size, rows, orbitals = vectors_ref.shape
    own = rows_upper[...].astype(f32) + rows_lower[...].astype(f32)
    vectors = vectors_ref[...].reshape(size * rows, orbitals)
    left = product(split(vectors), (upper[...], lower[...])).reshape(size, rows, orbitals)
    out_upper[...], out_lower[...] = split(left)
    diagonal[...] = jnp.sum(left * own[None], axis=1, keepdims=True)


def first_product(chol_vectors, step, me):
    vectors, rows, orbitals = chol_vectors.shape
    part = jax.ShapeDtypeStruct(chol_vectors.shape, bf16)
    block = pl.BlockSpec((quad, rows, orbitals), lambda i, me: (i, 0, 0))
    square = pl.BlockSpec(
        (orbitals, orbitals), lambda i, me: (0, 0), pipeline_mode=pl.Buffered(1)
    )
    own = pl.BlockSpec((rows, orbitals), lambda i, me: (me[0], 0))
    out = pl.pallas_call(
        first_product_kernel,
        grid_spec=pltpu.PrefetchScalarGridSpec(
            num_scalar_prefetch=1,
            grid=(vectors // quad,),
            in_specs=[block, square, square, own, own],
            out_specs=[block, block, pl.BlockSpec((quad, 1, orbitals), lambda i, me: (i, 0, 0))],
        ),
        out_shape=[part, part, jax.ShapeDtypeStruct((vectors, 1, orbitals), f32)],
        cost_estimate=cost(6 * chol_vectors.size * orbitals, 8 * chol_vectors.size),
        compiler_params=room(20),
        name="first_product",
    )(me, chol_vectors, *step, *step)
    return out[:2], out[2]


def pack_kernel(kept, me_ref, one, two, one_out, two_out):
    rows = one.shape[1]
    for source, out, blocks in ((one, one_out, kept[0]), (two, two_out, kept[1])):
        for j, k in enumerate(blocks):
            at = pl.ds(pl.multiple_of((me_ref[0] ^ k) * rows, rows), rows)
            out[:, :, j * rows : (j + 1) * rows] = source[:, :, at]


def pack(chol_vectors, me, kept, first, count):
    vectors, rows, orbitals = chol_vectors.shape
    width = len(kept[0]) * rows
    second = vectors // 2 + first
    out = pl.BlockSpec((2, rows, width), lambda i, me: (i, 0, 0))
    return pl.pallas_call(
        functools.partial(pack_kernel, kept),
        grid_spec=pltpu.PrefetchScalarGridSpec(
            num_scalar_prefetch=1,
            grid=(count // 2,),
            in_specs=[
                pl.BlockSpec((2, rows, orbitals), lambda i, me: (i + first // 2, 0, 0)),
                pl.BlockSpec((2, rows, orbitals), lambda i, me: (i + second // 2, 0, 0)),
            ],
            out_specs=[out, out],
        ),
        out_shape=[jax.ShapeDtypeStruct((count, rows, width), f32)] * 2,
        cost_estimate=cost(0, 16 * count * rows * orbitals),
        compiler_params=room(10),
        name="pack",
    )(me, chol_vectors, chol_vectors)


def siblings_kernel(me_ref, one, two, one_out, two_out):
    one_out[...] = one[...]
    two_out[...] = two[...]


def for_siblings(chol_vectors, me, bits):
    vectors, rows, _ = chol_vectors.shape
    steps = vectors // 2 // quad
    block = (quad, rows, rows)
    out = pl.BlockSpec(block, lambda i, me: (i, 0, 0))
    return pl.pallas_call(
        siblings_kernel,
        grid_spec=pltpu.PrefetchScalarGridSpec(
            num_scalar_prefetch=1,
            grid=(steps,),
            in_specs=[
                pl.BlockSpec(block, lambda i, me, s=s, b=b: (s * steps + i, 0, me[0] ^ b ^ 1))
                for s, b in enumerate(bits)
            ],
            out_specs=[out, out],
        ),
        out_shape=[jax.ShapeDtypeStruct((vectors // 2, rows, rows), f32)] * 2,
        cost_estimate=cost(0, 8 * vectors * rows * rows),
        compiler_params=room(6),
        name="for_siblings",
    )(me, chol_vectors, chol_vectors)


def turns(side, count):
    if side == 0:
        return lambda i: jnp.minimum(i, count - 1)
    return lambda i: jnp.maximum(i - count, 0)


def shared_pieces_kernel(bits, kept, me_ref, own, *refs):
    steps = len(refs) - 7 - 2 * len(bits) * len(bits)
    others, siblings, refs = refs[:steps], refs[steps : steps + 2], refs[steps + 2 :]
    (upper, lower), outs, (left_upper, left_lower, blocks) = refs[:2], refs[2:-3], refs[-3:]
    turn_count = steps // 2
    count, rows, orbitals = own.shape
    pair = orbitals // 4
    half = len(outs) // 2
    step = pl.program_id(0)
    size = count * rows
    me = me_ref[0]

    def put(block, start, column):
        at = pl.ds(pl.multiple_of(column * rows, rows), rows)
        here = pl.ds(start, block.shape[0])
        left_upper[here, at], left_lower[here, at] = split(block)

    left_upper[:size], left_lower[:size] = split(own[...].reshape(size, orbitals))
    for i, other in enumerate(others):
        @pl.when(step == i)
        def _():
            for j, k in enumerate(kept[i // turn_count]):
                block = other[:, :, j * rows : (j + 1) * rows].reshape(size, rows)
                put(block, size, me ^ bits[i // turn_count] ^ k)

    for side in range(2):
        @pl.when(step // turn_count == side)
        def _():
            at = pl.ds(pl.multiple_of((me ^ bits[side]) * rows, rows), rows)
            for p in range(count):
                put(own[p, :, at].T, size + p * rows, me)
                put(siblings[side][p].T, size + p * rows, me ^ 1)

    left = left_upper[...], left_lower[...]
    middle = pl.ds(pl.multiple_of((1 + step // turn_count) * pair, pair), pair)
    for n, at in enumerate((pl.ds(0, pair), middle)):
        value = product(left, (upper[:, at], lower[:, at]))
        for b in range(half // 2):
            for p in range(2 * count):
                block = value[p * rows : (p + 1) * rows, b * rows : (b + 1) * rows]
                blocks[n * (half // 2) + b, p % count, p // count] = block.T
    for side in range(2):
        @pl.when(step // turn_count == side)
        def _():
            for b in range(half):
                outs[side * half + b][...] = blocks[b]


def shared_pieces(bits, kept, near, me, chol_vectors, starts, others, siblings, right):
    _, rows, orbitals = chol_vectors.shape
    half = len(near[0])
    count = len(others) // 2
    first, second = (start // 2 for start in starts)
    specs = [
        pl.BlockSpec(
            (2, rows, orbitals),
            lambda i, me: (jnp.where(i < count, first + i, second + i - count), 0, 0),
        )
    ]
    for x, which in others:
        specs.append(
            pl.BlockSpec(
                (2,) + x.shape[1:], lambda i, me, w=which: (w, 0, 0), pipeline_mode=pl.Buffered(1)
            )
        )
    outs = []
    for side in range(2):
        turn_of = turns(side, count)
        specs.append(
            pl.BlockSpec((2, rows, rows), lambda i, me, t=turn_of: (first + t(i), 0, 0))
        )
        outs += [
            pl.BlockSpec((2, 2, rows, rows), lambda i, me, t=turn_of: (t(i), 0, 0, 0))
        ] * half
    square = pl.BlockSpec(
        (orbitals, orbitals), lambda i, me: (0, 0), pipeline_mode=pl.Buffered(1)
    )
    out = pl.pallas_call(
        functools.partial(shared_pieces_kernel, bits, kept),
        grid_spec=pltpu.PrefetchScalarGridSpec(
            num_scalar_prefetch=1,
            grid=(2 * count,),
            in_specs=specs + [square] * 2,
            out_specs=outs,
            scratch_shapes=[
                pltpu.VMEM((4 * rows, orbitals), bf16),
                pltpu.VMEM((4 * rows, orbitals), bf16),
                pltpu.VMEM((half, 2, 2, rows, rows), f32),
            ],
        ),
        out_shape=[jax.ShapeDtypeStruct((2 * count, 2, rows, rows), f32)] * (2 * half),
        cost_estimate=cost(
            24 * count * rows * orbitals**2, 32 * count * rows * orbitals
        ),
        compiler_params=room(30),
        name="shared_pieces",
    )(me, chol_vectors, *(x for x, _ in others), *siblings, *right)
    return out[:half], out[half:]


def shared_rotated_kernel(orders, upper, lower, *refs):
    out_ref, left_upper, left_lower = refs[-3:]
    count, rows, _ = out_ref.shape
    half = len(orders[0]) // 2
    for side, order in enumerate(orders):
        @pl.when(pl.program_id(0) * 2 // pl.num_programs(0) == side)
        def _():
            for k, (index, which) in enumerate(order):
                here = pl.ds(k * rows, rows)
                part = refs[side * half + index][:, which].reshape(count * rows, rows)
                left_upper[:, here], left_lower[:, here] = split(part)

    left = left_upper[...], left_lower[...]
    out_ref[...] = product(left, (upper[...], lower[...])).reshape(out_ref.shape)


def shared_rotated(previous, parts, orders, starts, right, shape):
    _, rows, orbitals = shape
    fresh = previous is None
    pairs = parts[0][0].shape[0] // 2
    first, second = (start // 2 for start in starts)
    specs = []
    for side in range(2):
        turn_of = turns(side, pairs)
        specs += [
            pl.BlockSpec((2, 2, rows, rows), lambda i, t=turn_of: (t(i), 0, 0, 0))
        ] * len(parts[side])
    count = 2 + len(specs)
    return pl.pallas_call(
        functools.partial(shared_rotated_kernel, orders),
        grid=(2 * pairs,),
        in_specs=[resident((orbitals, orbitals))] * 2
        + specs
        + ([] if fresh else [pl.BlockSpec(memory_space=pl.ANY)]),
        out_specs=pl.BlockSpec(
            (2, rows, orbitals), lambda i: (jnp.where(i < pairs, first + i, second + i - pairs), 0, 0)
        ),
        out_shape=jax.ShapeDtypeStruct(shape, f32),
        input_output_aliases={} if fresh else {count: 0},
        scratch_shapes=[pltpu.VMEM((2 * rows, orbitals), bf16)] * 2,
        cost_estimate=cost(24 * pairs * rows * orbitals**2, 32 * pairs * rows * orbitals),
        compiler_params=room(16),
        name="shared_rotated",
    )(*right, *parts[0], *parts[1], *([] if fresh else [previous]))


def second_terms_kernel(upper_ref, lower_ref, diagonal_ref, out_ref):
    total = jnp.zeros(out_ref.shape, f32)
    for p in range(upper_ref.shape[0]):
        left = upper_ref[p].astype(f32) + lower_ref[p].astype(f32)
        total = total + left * diagonal_ref[p]
    out_ref[...] = total


def second_terms(lefts, diagonal):
    vectors, rows, orbitals = lefts[0].shape
    size = 16
    block = pl.BlockSpec((vectors, size, orbitals), lambda i: (0, i, 0))
    return pl.pallas_call(
        second_terms_kernel,
        grid=(rows // size,),
        in_specs=[block, block, pl.BlockSpec((vectors, 1, orbitals), lambda i: (0, 0, 0))],
        out_specs=pl.BlockSpec((size, orbitals), lambda i: (i, 0)),
        out_shape=jax.ShapeDtypeStruct((rows, orbitals), f32),
        cost_estimate=cost(2 * lefts[0].size, 4 * lefts[0].size),
        compiler_params=room(8),
        name="second_terms",
    )(*lefts, diagonal)


def flip(x, k):
    count = lax.axis_size("vec")
    return lax.ppermute(x, "vec", [(i, i ^ k) for i in range(count)])


def sum_halves(part):
    bits = lax.axis_size("vec").bit_length() - 1
    masks = [2 ** (b + 1) - 1 for b in range(bits)]
    half = part.shape[0] // 2
    one, two = part[:half], part[half:]
    for a, b in zip(masks, reversed(masks)):
        one_more, two_more = flip(one, a), flip(two, b)
        one, two = one + one_more, two + two_more
    return one, two


def shards_of(one, two):
    high, low = lax.axis_size("row") // 2, lax.axis_size("row") // 4
    one_low, two_high = swap(one, low), swap(two, high)
    one_high, two_low = swap(one, high), swap(two, low)
    one_both, two_both = swap(one_low, high), swap(two_high, low)
    halves = {
        0: (one, two),
        low: (one_low, two_low),
        high: (one_high, two_high),
        low | high: (one_both, two_both),
    }
    out = []
    for k in sorted(halves):
        out += [*halves[k], *(swap(x, 1) for x in halves[k])]
    return out


def after(x, *others):
    return lax.optimization_barrier((x,) + others)[0]


def tiled_shards(chol_vectors):
    shape = chol_vectors.shape
    vectors, _, _ = shape
    devices = lax.axis_size("row")
    me = lax.axis_index("row").astype(jnp.int32)[None]
    middle = vectors // 2
    bits = (devices // 2, devices // 4)
    everyone = list(range(devices))
    near = [[k for k in everyone if not k & bit] for bit in bits]
    kept = [[k for k in everyone if k not in (bit, bit ^ 1)] for bit in bits]
    orders = [
        [(near[s].index(k & ~bit), int(bool(k & bit))) for k in everyone]
        for s, bit in enumerate(bits)
    ]

    eighth = middle // 8
    packed, place_of = [], []
    for part, count in enumerate((eighth, 3 * eighth, 2 * eighth, 2 * eighth)):
        start = len(place_of) * 2
        packed.append(pack(chol_vectors, me, kept, start, count))
        place_of += [(part, i) for i in range(count // 2)]
    blocks = for_siblings(chol_vectors, me, bits)
    early = []

    def send_early(*others):
        part = len(early)
        early.append(
            [swap(after(x, *others), bit) for x, bit in zip(packed[part], bits)]
        )

    part = gradient_terms(chol_vectors, me)
    halves = sum_halves(part)
    send_early()
    siblings = [swap(x, 1) for x in blocks]
    gathered = shards_of(*halves)
    send_early(*gathered)
    *step, turned_upper, turned_lower = make_step(first_kernel, me, gathered, (), 4)
    lefts, diagonal = first_product(chol_vectors, step, me)
    diagonal = sum_over_row(diagonal)
    send_early(diagonal)
    part = second_terms(lefts, diagonal)
    gathered = shards_of(*sum_halves(part))
    send_early(*gathered)
    next_step = make_step(second_kernel, me, gathered, (turned_upper, turned_lower), 2)
    by_column, by_row, rotation = compose(me, step, next_step, devices)

    last = len(place_of) - 1
    groups = [[0, 1], [2, 3, 4]] + [[h, h + 1] for h in range(5, last, 2)] + [[last]]
    starts = [(2 * group[0], middle + 2 * group[0]) for group in groups]
    parts = []

    for g, group in enumerate(groups):
        others = []
        for s in range(2):
            for h in group:
                window, which = place_of[h]
                others.append((early[window][s], which))
        sent = shared_pieces(
            bits, kept, near, me, chol_vectors, starts[g], others, siblings, by_column
        )
        parts.append(
            [
                [pieces[0]]
                + [swap(pieces[i], near[s][i]) for i in range(1, len(near[s]))]
                for s, pieces in enumerate(sent)
            ]
        )
        by_column = lax.optimization_barrier((*by_column, *sent[0], *sent[1]))[:2]
    rotated = None
    for g in range(len(groups)):
        rotated = shared_rotated(rotated, parts[g], orders, starts[g], by_row, shape)
    return rotated, rotation


def shards(chol_vectors):
    vectors, rows, _ = chol_vectors.shape
    devices, groups = lax.axis_size("row"), lax.axis_size("vec")
    tiled = rows % lane == 0 and vectors % (8 * quad) == 0 and devices == 8
    if tiled and groups & (groups - 1) == 0:
        return tiled_shards(chol_vectors)
    return plain_shards(chol_vectors)


def solution(mesh):
    return jax.shard_map(
        shards,
        mesh=mesh,
        in_specs=(P("vec", "row", None),),
        out_specs=(P("vec", "row", None), P("row", None)),
        check_vma=False,
    )
```
